32 devices in a mesh: gx: 4 (over y, x), gy: 4 (over z), gz: 2 (over core).
Axes of the slice: x: 2, y: 2, z: 4, core: 2. Of those that a mesh axis runs over, the one named last changes fastest.
Arguments:
- right_side: float32 [16, 256, 512], P('gz', 'gx', 'gy'), may hold values from -6 to 6
- permeability: float32 [16, 256, 512], P('gz', 'gx', 'gy'), may hold values from 0.05 to 50
- storage: float32 [16, 256, 512], P('gz', 'gx', 'gy'), may hold values from 0.05 to 0.5
- deflation: float32 [8, 16, 256, 512], P(None, 'gz', 'gx', 'gy'), may hold values from -0.0234375 to 0.0234375
- coarse_inverse: float32 [256, 256], P('gx'), as said below
- owners: int32 [2, 4, 4, 8], P('gz', 'gx', 'gy'), may hold values from 0 to 255, as said below
- margin: int32 [2, 4, 4, 6], P('gz', 'gx', 'gy'), may hold values from 0 to 1
Outputs:
- solution: float32 [16, 256, 512], P('gz', 'gx', 'gy')
- residual: float32 [16, 256, 512], P('gz', 'gx', 'gy')
The draws below stay inside these ranges and needn't reach their ends.
Inputs may be any that keep to these rules, and one draw needn't show every extreme that they name: `coarse_inverse`: symmetric and positive definite. `owners`: every coarse index appears exactly once.
All inputs are finite; a program needn't handle non-finite values.
Results may differ from the reference program's by a relative error of at most 0.0003.
Values sent between devices are 32-bit elements; how exact they have to be, the bound alone decides.
No kernel may reach another device: no remote copies, remote signals or barrier semaphores. Data moves between devices by JAX's collectives and lax.ppermute only.
A program may use at most 128 MiB of HBM per device.

```python
import math
import jax
import jax.numpy as jnp
from jax import lax

CZ = 8
CX = 64
CY = 128
NV = 8
SWEEPS = 2
ITERS = 4
NBZ = 2
NBX = 4
NBY = 4
NZ = 16
NX = 256
NY = 512
COARSE = 256
N_GX = 4
N_GY = 4
N_GZ = 2


def draw_coarse_inverse(key, part):
    noise_key = jax.random.fold_in(key, 11)
    diag_key = jax.random.fold_in(key, 12)
    noise_part = jax.random.normal(noise_key, (COARSE, COARSE), jnp.float32) * (0.4 / math.sqrt(2.0 * COARSE))
    diagonal = 1.0 + 0.2 * jax.random.uniform(diag_key, (COARSE,), jnp.float32)
    matrix = noise_part + noise_part.T + jnp.diag(diagonal)
    return matrix * (0.2 * math.sqrt(CZ * CX * CY / NV))


def draw_owners(key, part):
    shuffled = jax.random.permutation(jax.random.fold_in(key, 21), COARSE)
    return shuffled.astype(jnp.int32).reshape(NBZ, NBX, NBY, NV)


def draw_margin(key, part):
    depth_draw = jax.random.randint(jax.random.fold_in(key, 31), (NBZ, NBX, NBY, 6), 0, 2).astype(jnp.int32)
    depth_draw = depth_draw.at[0, 0, 0, 0].set(1)
    return depth_draw.at[0, 0, 0, 1].set(0)


def block_levels(key, extent, split, smallest, high):
    gain, own = 1.0, jax.random.fold_in(key, 6)
    for dim, shards_of in split:
        steps = jnp.exp(jax.random.uniform(jax.random.fold_in(own, dim), (shards_of,), jnp.float32, smallest / len(split), high / len(split)))
        gain = gain * jnp.repeat(steps, extent[dim] // shards_of).reshape([-1 if axis == dim else 1 for axis in range(len(extent))])
    return gain


def normal_values(key, shape, scale, limit, cuts=(), kind=jnp.bfloat16):
    entries = jax.random.normal(key, shape, jnp.float32) * scale
    if len(cuts) > 0:
        entries = block_levels(key, shape, cuts, -0.22, 0.18) * entries
    return jnp.clip(entries, min=-limit, max=limit).astype(kind)


def setup_inputs(seed: int = 0) -> dict:
    splits = jax.random.split(jax.random.key(seed), 8)
    return {
        "right_side": normal_values(splits[0], (NZ, NX, NY), 1.0, 6.0, ((0, 2), (1, 4), (2, 4)), jnp.float32),
        "permeability": jnp.clip(jnp.exp(math.log(50.0) - 6.9077553 * jax.random.uniform(splits[1], (NZ, NX, NY), jnp.float32) ** block_levels(splits[1], (NZ, NX, NY), ((0, 2), (1, 4), (2, 4)), -0.2, 0.2)), 0.05, 50.0),
        "storage": jnp.clip(jnp.exp(math.log(0.5) - 2.3025851 * jax.random.uniform(splits[2], (NZ, NX, NY), jnp.float32) ** block_levels(splits[2], (NZ, NX, NY), ((0, 2), (1, 4), (2, 4)), -0.2, 0.2)), 0.05, 0.5),
        "deflation": normal_values(splits[3], (NV, NZ, NX, NY), (CZ * CX * CY) ** -0.5, 0.0234375, ((1, 2), (2, 4), (3, 4)), jnp.float32),
        "coarse_inverse": draw_coarse_inverse(jax.random.fold_in(splits[7], 71), 0),
        "owners": draw_owners(jax.random.fold_in(splits[7], 71), 0),
        "margin": draw_margin(jax.random.fold_in(splits[7], 71), 0),
    }


RELAXATION = 0.7
PRECISE = lax.Precision.HIGHEST


def conduct(first_perm, second_perm):
    return 2.0 * first_perm * second_perm / jnp.maximum(first_perm + second_perm, 0.05)


def neighbour(padded, dimension, offset):
    starts = [1, 1, 1]
    starts[dimension] = 1 + offset
    limits = [starts[0] + padded.shape[0] - 2, starts[1] + padded.shape[1] - 2, starts[2] + padded.shape[2] - 2]
    return lax.slice(padded, starts, limits)


def diagonal_of(perm_pad, storage_in):
    perm_center = neighbour(perm_pad, 0, 0)
    diagonal = storage_in
    for dimension in range(3):
        for offset in (-1, 1):
            diagonal = diagonal + conduct(perm_center, neighbour(perm_pad, dimension, offset))
    return diagonal


def stencil(padded, perm_pad, storage_in):
    center = neighbour(padded, 0, 0)
    perm_center = neighbour(perm_pad, 0, 0)
    applied = storage_in * center
    for dimension in range(3):
        for offset in (-1, 1):
            transmit = conduct(perm_center, neighbour(perm_pad, dimension, offset))
            applied = applied + transmit * (center - neighbour(padded, dimension, offset))
    return applied


def line_mask(length, low_side, high_side, position, blocks):
    places = jnp.arange(length + 2, dtype=jnp.int32)
    inside = (places >= 1 - low_side) & (places <= length + high_side)
    ingrid = ((places >= 1) | (position > 0)) & ((places <= length) | (position < blocks - 1))
    return (inside & ingrid).astype(jnp.float32)


def local_solve(residual_ext, perm_pad, storage_ext, keep_mask, inverse):
    source = keep_mask * residual_ext
    solved = RELAXATION * inverse * source
    for sweep_count in range(SWEEPS - 1):
        applied = stencil(jnp.pad(solved, 1), perm_pad, storage_ext)
        solved = solved + RELAXATION * inverse * (source - applied)
    return solved[1:-1, 1:-1, 1:-1]


def reference(right_side, permeability, storage, deflation, coarse_inverse, owners, margin):
    perm_pad2 = jnp.pad(permeability, 2)
    perm_pad1 = jnp.pad(permeability, 1)
    storage_pad = jnp.pad(storage, 1)
    vector_blocks = deflation.reshape(NV, N_GZ, CZ, N_GX, CX, N_GY, CY)

    def schwarz_local(residual):
        residual_pad = jnp.pad(residual, 1)

        def one_block(flat_index):
            brick_z = flat_index // (N_GX * N_GY)
            brick_x = (flat_index // N_GY) % N_GX
            brick_y = flat_index % N_GY
            starts = (brick_z * CZ, brick_x * CX, brick_y * CY)
            residual_ext = lax.dynamic_slice(residual_pad, starts, (CZ + 2, CX + 2, CY + 2))
            perm_ext = lax.dynamic_slice(perm_pad2, starts, (CZ + 4, CX + 4, CY + 4))
            storage_ext = lax.dynamic_slice(storage_pad, starts, (CZ + 2, CX + 2, CY + 2))
            depths = margin[brick_z, brick_x, brick_y]
            keep_mask = (line_mask(CZ, depths[0], depths[1], brick_z, N_GZ)[:, None, None]
                         * line_mask(CX, depths[2], depths[3], brick_x, N_GX)[None, :, None]
                         * line_mask(CY, depths[4], depths[5], brick_y, N_GY)[None, None, :])
            diagonal = diagonal_of(perm_ext, storage_ext)
            inverse = keep_mask / jnp.where(keep_mask > 0, diagonal, 1.0)
            return local_solve(residual_ext, perm_ext, storage_ext, keep_mask, inverse)

        pieces = lax.map(one_block, jnp.arange(N_GZ * N_GX * N_GY, dtype=jnp.int32))
        pieces = pieces.reshape(N_GZ, N_GX, N_GY, CZ, CX, CY).transpose(0, 3, 1, 4, 2, 5)
        return pieces.reshape(NZ, NX, NY)

    def coarse_part(residual):
        residual_blocks = residual.reshape(N_GZ, CZ, N_GX, CX, N_GY, CY)
        coefficients = jnp.einsum('kaibjcl,aibjcl->abck', vector_blocks, residual_blocks, precision=PRECISE)
        vector = jnp.zeros((COARSE,), jnp.float32).at[owners.reshape(-1)].set(coefficients.reshape(-1))
        solved = jnp.dot(coarse_inverse, vector, precision=PRECISE)
        picked = solved[owners]
        correction = jnp.einsum('kaibjcl,abck->aibjcl', vector_blocks, picked, precision=PRECISE)
        return correction.reshape(NZ, NX, NY)

    def precondition(residual):
        return schwarz_local(residual) + coarse_part(residual)

    def operate(direction):
        return stencil(jnp.pad(direction, 1), perm_pad1, storage)

    solution = jnp.zeros((NZ, NX, NY), jnp.float32)
    residual = right_side
    precond = precondition(residual)
    direction = precond
    inner_prod = jnp.sum(residual * precond)
    for iteration in range(ITERS):
        applied = operate(direction)
        step_size = inner_prod / jnp.sum(direction * applied)
        solution = solution + step_size * direction
        residual = residual - step_size * applied
        if iteration + 1 < ITERS:
            precond = precondition(residual)
            fresh_prod = jnp.sum(residual * precond)
            direction = precond + (fresh_prod / inner_prod) * direction
            inner_prod = fresh_prod
    return (solution, residual)
```

```python
import jax
import jax.numpy as jnp
from jax import lax
from jax.sharding import PartitionSpec as P

ITERS = 4
RELAXATION = 0.7
PRECISE = lax.Precision.HIGHEST
AXES = ("gx", "gy", "gz")
SIDES = (("gz", 0), ("gx", 1), ("gy", 2))


def conduct(first_perm, second_perm):
    return 2.0 * first_perm * second_perm / jnp.maximum(first_perm + second_perm, 0.05)


def faces(cells):
    out = []
    for axis, dim in SIDES:
        count = lax.axis_size(axis)
        head = lax.slice_in_dim(cells, 0, 1, axis=dim)
        tail = lax.slice_in_dim(cells, cells.shape[dim] - 1, cells.shape[dim], axis=dim)
        low = lax.ppermute(tail, axis, [(i, i + 1) for i in range(count - 1)])
        high = lax.ppermute(head, axis, [(i + 1, i) for i in range(count - 1)])
        out.append((low, high))
    return out


def extended(cells, halo, dim):
    return jnp.concatenate([halo[0], cells, halo[1]], axis=dim)


def couplings(cells, halos, transmit, scale=None):
    total = 0.0
    for dim in range(3):
        low, high = halos[dim]
        if scale is not None:
            low, high = low * scale[2 * dim], high * scale[2 * dim + 1]
        size = cells.shape[dim]
        padded = extended(cells, (low, high), dim)
        before = lax.slice_in_dim(padded, 0, size, axis=dim)
        after = lax.slice_in_dim(padded, 2, size + 2, axis=dim)
        t = transmit[dim]
        total = total + lax.slice_in_dim(t, 0, size, axis=dim) * before
        total = total + lax.slice_in_dim(t, 1, size + 1, axis=dim) * after
    return total


def everyone(row):
    count = 1
    for axis in AXES:
        count *= lax.axis_size(axis)
    copies = jnp.broadcast_to(row[None], (count,) + row.shape)
    return lax.all_to_all(copies, AXES, 0, 0, tiled=True)


def local(right_side, permeability, storage, deflation, coarse_inverse, owners, margin):
    vectors = deflation.shape[0]
    order = coarse_inverse.shape[1]
    depths = margin.reshape(6).astype(jnp.float32)
    sizes = [lax.axis_size(a) for a in AXES]
    me = (lax.axis_index("gx") * sizes[1] + lax.axis_index("gy")) * sizes[2] + lax.axis_index("gz")

    def coefficients(field):
        return jnp.sum(deflation * field[None], axis=(1, 2, 3))

    perm_faces = faces(permeability)
    transmit, diagonal = [], storage
    for dim in range(3):
        size = permeability.shape[dim]
        padded = extended(permeability, perm_faces[dim], dim)
        t = conduct(
            lax.slice_in_dim(padded, 0, size + 1, axis=dim),
            lax.slice_in_dim(padded, 1, size + 2, axis=dim),
        )
        transmit.append(t)
        diagonal = diagonal + lax.slice_in_dim(t, 0, size, axis=dim)
        diagonal = diagonal + lax.slice_in_dim(t, 1, size + 1, axis=dim)
    relax = RELAXATION / diagonal

    first = jnp.concatenate([coefficients(right_side), owners.reshape(-1).astype(jnp.float32)])
    table = everyone(first)
    known = table[:, :vectors].reshape(-1)
    owner_all = table[:, vectors:].reshape(-1)
    picker = (owner_all[:, None] == jnp.arange(order, dtype=jnp.float32)[None, :]).astype(jnp.float32)
    whole = lax.all_gather(coarse_inverse, "gx", axis=0, tiled=True)
    whole = jnp.dot(jnp.dot(picker, whole, precision=PRECISE), picker.T, precision=PRECISE)

    def precondition(residual, vector):
        scaled = relax * residual
        smooth = (2.0 - RELAXATION) * scaled + relax * couplings(scaled, faces(scaled), transmit, depths)
        solved = jnp.dot(whole, vector, precision=PRECISE)
        mine = lax.dynamic_slice(solved, (me * vectors,), (vectors,))
        return smooth + jnp.sum(deflation * mine[:, None, None, None], axis=0)

    def operate(field):
        return diagonal * field - couplings(field, faces(field), transmit)

    solution = jnp.zeros(right_side.shape, jnp.float32)
    residual = right_side
    direction = image = solution
    image_known = jnp.zeros_like(known)
    old_inner = jnp.float32(1.0)
    curvature = jnp.float32(0.0)
    for iteration in range(ITERS):
        precond = precondition(residual, known)
        applied = operate(precond)
        scalars = jnp.stack(
            [jnp.sum(residual * precond), jnp.sum(precond * applied), jnp.sum(precond * image)]
        )
        parts = everyone(jnp.concatenate([scalars, coefficients(applied)]))
        sums = jnp.sum(parts[:, :3], axis=0)
        inner = sums[0]
        ratio = inner / old_inner if iteration else jnp.float32(0.0)
        curvature = sums[1] + ratio * (2.0 * sums[2] + ratio * curvature)
        step = inner / curvature
        direction = precond + ratio * direction
        image = applied + ratio * image
        image_known = parts[:, 3:].reshape(-1) + ratio * image_known
        solution = solution + step * direction
        residual = residual - step * image
        known = known - step * image_known
        old_inner = inner
    return (solution, residual)


def solution(mesh):
    in_specs = (
        P("gz", "gx", "gy"),
        P("gz", "gx", "gy"),
        P("gz", "gx", "gy"),
        P(None, "gz", "gx", "gy"),
        P("gx", None),
        P("gz", "gx", "gy", None),
        P("gz", "gx", "gy", None),
    )
    out_specs = (P("gz", "gx", "gy"), P("gz", "gx", "gy"))
    return jax.shard_map(local, mesh=mesh, in_specs=in_specs, out_specs=out_specs, check_vma=False)
```

```python
import jax
import jax.numpy as jnp
from jax import lax
from jax.experimental import pallas as pl
from jax.experimental.pallas import tpu as pltpu
from jax.sharding import PartitionSpec as P

ITERS = 4
RELAXATION = 0.7
PRECISE = lax.Precision.HIGHEST
LANES = 128
STRIDE = 8
PERIOD = 32
ROW = 32
SLOT = 40


def conduct(first_perm, second_perm):
    return 2.0 * first_perm * second_perm / jnp.maximum(first_perm + second_perm, 0.05)


def turn(values, shift, axis):
    size = values.shape[axis]
    if isinstance(shift, int):
        shift = shift % size
        if shift == 0:
            return values
    return pltpu.roll(values, shift, axis)


def x_next(v):
    return turn(v, -1, 0)


def x_prev(v):
    return turn(v, 1, 0)


def y_next(v):
    return turn(v, -1, 1)


def y_prev(v):
    return turn(v, 1, 1)


def iota(shape, dim):
    return lax.broadcasted_iota(jnp.int32, shape, dim)


def place(shape):
    lane = iota(shape, 1)
    return lane >> 3, lane & 7


def eights(values):
    out = values[0:8]
    for t in range(1, values.shape[0] // 8):
        out = out + values[8 * t : 8 * t + 8]
    return out


def pack_kernel(zdim, xdim, *refs):
    (own, other) = (refs[0:3], refs[3:6])
    (hi_own, lo_own, hi_other, lo_other, d_own, d_other) = refs[6:12]
    main, strip_hi, strip_lo = refs[12:15]
    rows = xdim + 8
    shape = (rows, LANES)
    plane_of, slot_of = place(shape)
    for f in range(3):
        acc = jnp.zeros(shape, jnp.float32)
        for p in range(2 * zdim):
            pz = p % zdim
            src = own if p < zdim else other
            hi = hi_own if p < zdim else hi_other
            lo = lo_own if p < zdim else lo_other
            at = (f * zdim + pz) * 3
            tile = jnp.concatenate(
                [hi[at : at + 3, :], jnp.zeros((2, LANES), jnp.float32), lo[at : at + 3, :]], axis=0
            )
            plane = jnp.concatenate([src[f][pz], tile], axis=0)
            main[f, p] = plane
            moved = turn(plane, STRIDE * p + 3, 1)
            acc = jnp.where((plane_of == p) & (slot_of < 6), moved, acc)
        strip_hi[f * rows : (f + 1) * rows, :] = acc
        strip_lo[f * rows : (f + 1) * rows, :] = acc
    lane = iota((xdim, LANES), 1)
    vectors = d_own.shape[0]
    hi_acc = jnp.zeros((xdim, LANES), jnp.float32)
    lo_acc = hi_acc
    for b, d_ref in ((0, d_own), (1, d_other)):
        for k in range(vectors):

            def body(pz, carry, k=k, b=b, d_ref=d_ref):
                one, two = carry
                at = STRIDE * (b * zdim + pz) + k
                moved = pltpu.roll(d_ref[k, pz], at + 1, 1)
                one = jnp.where(lane == at, moved, one)
                two = jnp.where(lane == ((at + 1) & (LANES - 1)), moved, two)
                return one, two

            hi_acc, lo_acc = lax.fori_loop(0, zdim, body, (hi_acc, lo_acc))
    strip_hi[3 * rows : 3 * rows + xdim, :] = hi_acc
    strip_lo[3 * rows : 3 * rows + xdim, :] = turn(lo_acc, -1, 1)


def solve_coarse(known, select_ref, yb_ref):
    total = 0.0
    for t, row in enumerate(known):
        total = total + select_ref[:, LANES * t : LANES * (t + 1)] * row
    column = jnp.sum(total, axis=1, keepdims=True)
    yb_ref[...] = jnp.broadcast_to(column, yb_ref.shape)


def finish(c, scaled, strip_q, r_ref, z_ref, send_ref, w_ref, zown_ref, sw_ref, img_ref, ids, last):
    zdim, xdim = c["d_own"].shape[1], c["d_own"].shape[2]
    planes, rows = 2 * zdim, xdim + 8
    vectors = c["d_own"].shape[0]
    strips = c["strips"]
    yb = c["yb"]
    plane_of, slot_of = place((rows, LANES))

    te, cxp, cxm, cin, cout, czp, czm, ss = (strips[i] for i in range(8))
    smooth = (
        cxp * x_next(strip_q)
        + cxm * x_prev(strip_q)
        + cin * turn(strip_q, 4, 1)
        + cout * turn(strip_q, 2, 1)
        + czp * turn(strip_q, -STRIDE, 1)
        + czm * turn(strip_q, STRIDE, 1)
    )
    strip_z = (2.0 - RELAXATION) * strip_q + ss * smooth
    lane16 = iota((2 * vectors, LANES), 1)
    row16 = iota((2 * vectors, LANES), 0)
    wanted = row16 == (lane16 >> 6) * vectors + (lane16 & 7)
    for side, d_strip in ((0, c["dy_hi"]), (1, c["dy_lo"])):
        at = 6 * vectors + side * 2 * vectors
        coeff = jnp.sum(jnp.where(wanted, yb[at : at + 2 * vectors, :], 0.0), axis=0, keepdims=True)
        t = d_strip[...] * coeff
        t = t + turn(t, -1, 1)
        t = t + turn(t, -2, 1)
        t = t + turn(t, -4, 1)
        t = jnp.where(slot_of[:xdim] == 5 + side, turn(t, 5 + side, 1), 0.0)
        t = jnp.concatenate([t, jnp.zeros((8, LANES), jnp.float32)], axis=0)
        strip_z = strip_z + t
    edge_q = te * strip_q
    edge_z = te * strip_z

    row8 = iota((8, LANES), 0)
    for b in range(2):
        d_ref = c["d_own"] if b == 0 else c["d_other"]
        x_rows = []
        for side in range(2):
            dx = c["dx"][2 * b + side]
            acc = 0.0
            for k in range(vectors):
                at = (3 * b + 1 + side) * vectors + k
                acc = acc + dx[k * zdim : (k + 1) * zdim, :] * yb[at : at + 1, :]
            x_rows.append(acc)
        c["bx"][0] = x_rows[0]
        c["bx"][1] = x_rows[1]
        mxp, mxm, my = c["mxp"][b], c["mxm"][b], c["my"][b]

        def body(pz, carry, b=b, d_ref=d_ref, mxp=mxp, mxm=mxm, my=my):
            p = b * zdim + pz
            q = scaled[p]
            tx, ty = c["tx"][p], c["ty"][p]
            acc = tx * mxp * x_next(q) + mxm * x_prev(tx * q)
            acc = acc + ty * y_next(q) + y_prev(ty * q)
            acc = acc + my * pltpu.roll(edge_q, LANES - 6 - STRIDE * p, 1)
            acc = acc + c["tzlp"][p] * scaled[lax.rem(p + 1, planes)]
            acc = acc + c["tzlm"][p] * scaled[lax.rem(p + planes - 1, planes)]
            z = (2.0 - RELAXATION) * q + c["s"][p] * acc
            field = 0.0
            for k in range(vectors):
                at = 3 * b * vectors + k
                field = field + d_ref[k, pz] * yb[at : at + 1, :]
            tile = jnp.where(row8 == 0, c["bx"][0, pl.ds(pz, 1), :], 0.0)
            tile = jnp.where(row8 == 7, c["bx"][1, pl.ds(pz, 1), :], tile)
            z = z + jnp.concatenate([field, tile], axis=0)
            z_ref[p] = z
            if b == 0:
                zown_ref[pz] = z[:xdim]
            return carry

        lax.fori_loop(0, zdim, body, 0)

    lane = iota((rows, LANES), 1)
    edge = jnp.where((lane == 0) | (lane == LANES - 1), 1.0, 0.0)
    plane64, slot64 = plane_of[:xdim], slot_of[:xdim]
    zero = jnp.zeros((8, LANES), jnp.float32)
    scal = (zero, zero, zero)
    coeffs = []
    packed = jnp.zeros((xdim, LANES), jnp.float32)
    for b in range(2):
        d_ref = c["d_own"] if b == 0 else c["d_other"]

        def body(pz, carry, b=b, d_ref=d_ref):
            scal, sums, packed = carry
            p = b * zdim + pz
            z = z_ref[p]
            tx, ty = c["tx"][p], c["ty"][p]
            before = lax.rem(p + planes - 1, planes)
            acc = tx * x_next(z) + x_prev(tx * z)
            acc = acc + ty * y_next(z) + y_prev(ty * z)
            acc = acc + edge * pltpu.roll(edge_z, LANES - 6 - STRIDE * p, 1)
            acc = acc + c["tz"][p] * z_ref[lax.rem(p + 1, planes)]
            acc = acc + c["tz"][before] * z_ref[before]
            w = (c["diag"][p] * z - acc)[:xdim]
            z = z[:xdim]
            w_ref[p] = w
            rz, zw, zi = scal
            rz = rz + eights(r_ref[p][:xdim] * z)
            zw = zw + eights(w * z)
            if img_ref is not None:
                zi = zi + eights(img_ref[p][:xdim] * z)
            sums = tuple(sums[k] + eights(d_ref[k, pz] * w) for k in range(vectors))
            moved = pltpu.roll(w, lax.rem(STRIDE * p + 2, LANES), 1)
            packed = jnp.where((plane64 == p) & (slot64 < 4), moved, packed)
            return (rz, zw, zi), sums, packed

        scal, sums, packed = lax.fori_loop(0, zdim, body, (scal, (zero,) * vectors, packed))
        coeffs.extend(sums)

    acc_ref = c["acc"]
    acc_ref[...] = jnp.zeros(acc_ref.shape, jnp.float32)
    for j, value in enumerate(coeffs + list(scal)):
        acc_ref[j : j + 1, :] = jnp.sum(value, axis=0, keepdims=True)
    column = jnp.sum(acc_ref[...], axis=1, keepdims=True)
    spread = jnp.broadcast_to(column, (PERIOD, LANES))
    spread = jnp.where(iota((PERIOD, LANES), 0) == (iota((PERIOD, LANES), 1) & (PERIOD - 1)), spread, 0.0)
    row = jnp.sum(spread, axis=0, keepdims=True)
    peers = send_ref.shape[0]
    if last:
        for p in range(peers):
            send_ref[p] = row
        return
    for p in range(peers):
        send_ref[p, ROW : ROW + 1, :] = row
    sw_ref[...] = packed
    for p in range(planes):
        send_ref[ids[1], 2 * p : 2 * p + 2, :] = w_ref[p, xdim - 2 : xdim, :]
        send_ref[ids[2], 2 * p : 2 * p + 2, :] = w_ref[p, 0:2, :]
    part = xdim // 4
    pair = (iota((part, LANES), 1) & 7) >> 1
    to_hi = jnp.zeros((part, LANES), jnp.float32)
    to_lo = to_hi
    for g in range(4):
        rows_g = packed[g * part : (g + 1) * part]
        to_hi = jnp.where(pair == g, turn(rows_g, 2 * g, 1), to_hi)
        to_lo = jnp.where(pair == g, turn(rows_g, 2 * g - 2, 1), to_lo)
    send_ref[ids[3], 0:part, :] = to_hi
    send_ref[ids[4], 0:part, :] = to_lo
    for i in (5, 6):
        send_ref[ids[i], 0:1, :] = packed[xdim - 1 : xdim, :]
    for i in (7, 8):
        send_ref[ids[i], 0:1, :] = packed[0:1, :]


def first_kernel(zdim, xdim, *refs):
    (ids, mt, f, s_own, s_hi, s_lo, d_own, d_other) = refs[0:8]
    dx = refs[8:12]
    (select, known_ref) = refs[12:14]
    (send, w_ref, zown, sw, strips, tx, ty, tz, tzlp, tzlm, s_ref, diag_ref, mxp, mxm, my, rs_ref) = refs[14:30]
    (scaled, z_ref, yb, acc, bx) = refs[30:35]
    planes, rows = 2 * zdim, xdim + 8
    shape = (rows, LANES)
    row, lane = iota(shape, 0), iota(shape, 1)
    plane_of, slot_of = place(shape)
    zb = ids[9]
    cut = jnp.where(zb == 0, planes - 1, zdim - 1)

    def mg(col, b, d):
        return mt[(col * 2 + b) * 6 + d]

    def by_row(b, d):
        return jnp.where(row < xdim, mg(0, b, d), jnp.where(row < xdim + 4, mg(1, b, d), mg(2, b, d)))

    for b in range(2):
        mxp[b] = jnp.where(row == xdim - 1, mg(0, b, 3), jnp.where(row == rows - 1, mg(2, b, 3), 1.0))
        mxm[b] = jnp.where(row == 0, mg(0, b, 2), jnp.where(row == xdim, mg(1, b, 2), 1.0))
        my[b] = jnp.where(lane == LANES - 1, by_row(b, 5), jnp.where(lane == 0, by_row(b, 4), 0.0))

    def strip(i):
        at = slice(i * rows, (i + 1) * rows)
        own, hi, lo = s_own[at, :], s_hi[at, :], s_lo[at, :]
        out = jnp.where((slot_of == 1) | (slot_of == 2), turn(own, -1, 1), 0.0)
        out = jnp.where(slot_of == 5, turn(hi, 2, 1), out)
        out = jnp.where(slot_of == 3, turn(hi, -1, 1), out)
        out = jnp.where(slot_of == 0, turn(hi, -5, 1), out)
        out = jnp.where(slot_of == 6, turn(lo, 4, 1), out)
        out = jnp.where(slot_of == 4, turn(lo, 3, 1), out)
        return jnp.where(slot_of == 7, turn(lo, 7, 1), out)

    ps, st, rs = strip(0), strip(1), strip(2)
    rs_ref[...] = rs
    face = (slot_of == 5) | (slot_of == 6)
    t_x = conduct(ps, x_next(ps))
    t_z = jnp.where(plane_of == cut, 0.0, conduct(ps, turn(ps, -STRIDE, 1)))
    t_in = jnp.where(face, conduct(ps, turn(ps, 4, 1)), 0.0)
    t_out = jnp.where(face, conduct(ps, turn(ps, 2, 1)), 0.0)
    t_far = jnp.where(
        slot_of == 3,
        conduct(ps, turn(ps, 3, 1)),
        jnp.where(slot_of == 4, conduct(ps, turn(ps, -3, 1)), 0.0),
    )
    diag_s = st + t_x + x_prev(t_x) + t_z + turn(t_z, STRIDE, 1)
    diag_s = diag_s + t_in + t_out + turn(t_out, -2, 1) + t_far
    ss = jnp.where(diag_s > 0.0, RELAXATION / jnp.where(diag_s > 0.0, diag_s, 1.0), 0.0)

    def by_side(b, d_hi, d_lo):
        return jnp.where(slot_of == 5, mg(3, b, d_hi), mg(4, b, d_lo))

    def by_brick(d_hi, d_lo):
        return jnp.where(plane_of < zdim, by_side(0, d_hi, d_lo), by_side(1, d_hi, d_lo))

    def only(values):
        return jnp.where(face, values, 0.0)

    strips[0] = t_in
    strips[1] = only(t_x * jnp.where(row == xdim - 1, by_brick(3, 3), 1.0))
    strips[2] = only(x_prev(t_x) * jnp.where(row == 0, by_brick(2, 2), 1.0))
    strips[3] = t_in * by_brick(4, 5)
    strips[4] = t_out
    high = (plane_of == zdim - 1) | (plane_of == planes - 1)
    low = (plane_of == 0) | (plane_of == zdim)
    strips[5] = only(t_z * jnp.where(high, by_brick(1, 1), 1.0))
    strips[6] = only(turn(t_z, STRIDE, 1) * jnp.where(low, by_brick(0, 0), 1.0))

    inside = lane < LANES - 1

    def transmit(p, carry):
        here = f[0, p]
        after = f[0, lax.rem(p + 1, planes)]
        tx[p] = conduct(here, x_next(here))
        ty[p] = jnp.where(inside, conduct(here, y_next(here)), 0.0)
        tz[p] = conduct(here, after) * jnp.where(p == cut, 0.0, 1.0)
        return carry

    lax.fori_loop(0, planes, transmit, 0)
    edge = (lane == 0) | (lane == LANES - 1)
    inner = jnp.zeros(shape, jnp.float32)
    for b in range(2):
        m_hi, m_lo = by_row(b, 1), by_row(b, 0)

        def diagonal(pz, inner, b=b, m_hi=m_hi, m_lo=m_lo):
            p = b * zdim + pz
            t_x, t_y, t_z = tx[p], ty[p], tz[p]
            t_b = tz[lax.rem(p + planes - 1, planes)]
            total = f[1, p] + t_x + x_prev(t_x) + t_y + y_prev(t_y) + t_z + t_b
            total = total + jnp.where(edge, pltpu.roll(t_in, LANES - 6 - STRIDE * p, 1), 0.0)
            relax = jnp.where(total > 0.0, RELAXATION / jnp.where(total > 0.0, total, 1.0), 0.0)
            diag_ref[p] = total
            s_ref[p] = relax
            tzlp[p] = t_z * jnp.where(pz == zdim - 1, m_hi, 1.0)
            tzlm[p] = t_b * jnp.where(pz == 0, m_lo, 1.0)
            scaled[p] = relax * f[2, p]
            moved = pltpu.roll(relax, lax.rem(STRIDE * p + 2, LANES), 1)
            return jnp.where((plane_of == p) & ((slot_of == 1) | (slot_of == 2)), moved, inner)

        inner = lax.fori_loop(0, zdim, diagonal, inner)
    ss = jnp.where((slot_of == 1) | (slot_of == 2), inner, ss)
    strips[7] = ss

    known = [known_ref[t : t + 1, :] for t in range(known_ref.shape[0])]
    solve_coarse(known, select, yb)
    c = dict(
        tx=tx, ty=ty, tz=tz, tzlp=tzlp, tzlm=tzlm, s=s_ref, diag=diag_ref, mxp=mxp, mxm=mxm, my=my,
        strips=strips, d_own=d_own, d_other=d_other, dx=dx, dy_hi=s_hi.at[3 * rows : 3 * rows + xdim, :],
        dy_lo=s_lo.at[3 * rows : 3 * rows + xdim, :], yb=yb, acc=acc, bx=bx,
    )
    finish(c, scaled, ss * rs, f.at[2], z_ref, send, w_ref, zown, sw, None, ids, False)


def totals(rows):
    lane = iota((1, LANES), 1)
    group = lane >> 5
    tiles = []
    for t in range(len(rows) // 4):
        tile = 0.0
        for i in range(4):
            tile = tile + jnp.where(group == i, rows[4 * t + i], 0.0)
        tiles.append(tile)
    total = tiles[0]
    for tile in tiles[1:]:
        total = total + tile
    index = lane & (PERIOD - 1)
    sums = [
        jnp.sum(jnp.where(index == 16 + j, total, 0.0), axis=1, keepdims=True) for j in range(3)
    ]
    return tiles, sums


def scalars(sums, scal_ref, first):
    inner = sums[0]
    if first:
        ratio = jnp.zeros_like(inner)
        curvature = sums[1]
    else:
        ratio = inner / scal_ref[0:1, 0:1]
        curvature = sums[1] + ratio * (2.0 * sums[2] + ratio * scal_ref[1:2, 0:1])
    return inner, ratio, curvature, inner / curvature


def next_kernel(zdim, xdim, first, last, *refs):
    refs = list(refs)

    def take(n):
        out, refs[:n] = refs[:n], []
        return out

    ids, got, d_own, d_other, *dx = take(8)
    s_hi, s_lo, select, strips, tx, ty, tz, tzlp, tzlm, s_ref, diag_ref, mxp, mxm, my = take(14)
    known_ref, w_in, z_in, sw_in, rs_in = take(5)
    if first:
        (f,) = take(1)
        r_in = f.at[2]
    else:
        r_in, img_in, dir_in, sol_in, is_in, kimg_ref, scal_ref = take(7)
    send, w_ref, zown, sw, rs_ref, r_ref, img_ref, dir_ref, sol_ref, is_ref, known_out, kimg_out, scal_out = take(13)
    scaled, z_ref, yb, acc, bx, tiles_ref = take(6)
    planes, rows = 2 * zdim, xdim + 8
    plane_of, slot_of = place((rows, LANES))

    peers = got.shape[0]
    tiles, sums = totals([got[p, ROW : ROW + 1, :] for p in range(peers)])
    inner, ratio, curvature, step = scalars(sums, None if first else scal_ref, first)
    scal_out[0:1, :] = jnp.broadcast_to(inner, (1, LANES))
    scal_out[1:2, :] = jnp.broadcast_to(curvature, (1, LANES))
    known = []
    for t, tile in enumerate(tiles):
        if not first:
            tile = tile + ratio * kimg_ref[t : t + 1, :]
        kimg_out[t : t + 1, :] = tile
        value = known_ref[t : t + 1, :] - step * tile
        known_out[t : t + 1, :] = value
        known.append(value)
    solve_coarse(known, select, yb)

    part = xdim // 4
    from_hi, from_lo = got[ids[3], 0:part, :], got[ids[4], 0:part, :]
    own = sw_in[...]
    slot_part = slot_of[:part]
    blocks = []
    for g in range(4):
        value = own[g * part : (g + 1) * part]
        value = jnp.where(slot_part == 5, turn(from_hi, 5 - 2 * g, 1), value)
        value = jnp.where(slot_part == 3, turn(from_hi, 2 - 2 * g, 1), value)
        value = jnp.where(slot_part == 4, turn(from_lo, 4 - 2 * g, 1), value)
        value = jnp.where(slot_part == 6, turn(from_lo, 5 - 2 * g, 1), value)
        blocks.append(value)
    slot8, row8 = slot_of[:8], iota((8, LANES), 0)
    tile = jnp.zeros((8, LANES), jnp.float32)
    for i, at, want, shift in ((5, 0, 5, 3), (6, 0, 6, 5), (7, 7, 5, 3), (8, 7, 6, 5)):
        value = turn(jnp.broadcast_to(got[ids[i], 0:1, :], (8, LANES)), shift, 1)
        tile = jnp.where((row8 == at) & (slot8 == want), value, tile)
    ws = jnp.concatenate(blocks + [tile], axis=0)
    ws = jnp.where((slot_of == 0) | (slot_of == 7), 0.0, ws)
    if not first:
        ws = ws + ratio * is_in[...]
    is_ref[...] = ws
    rs = rs_in[...] - step * ws
    rs_ref[...] = rs
    strip_q = strips[7] * rs

    tiles_ref[...] = jnp.zeros(tiles_ref.shape, jnp.float32)
    for p in range(planes):
        tiles_ref[p, 0:2, :] = got[ids[1], 2 * p : 2 * p + 2, :]
        tiles_ref[p, 6:8, :] = got[ids[2], 2 * p : 2 * p + 2, :]

    def update(p, carry):
        image = jnp.concatenate([w_in[p], tiles_ref[p]], axis=0)
        if not first:
            image = image + ratio * img_in[p]
        img_ref[p] = image
        r = r_in[p] - step * image
        r_ref[p] = r
        scaled[p] = s_ref[p] * r
        return carry

    lax.fori_loop(0, planes, update, 0)

    def advance(p, carry):
        d = z_in[p]
        if first:
            sol_ref[p] = step * d
        else:
            d = d + ratio * dir_in[p]
            sol_ref[p] = sol_in[p] + step * d
        dir_ref[p] = d
        return carry

    lax.fori_loop(0, zdim, advance, 0)
    c = dict(
        tx=tx, ty=ty, tz=tz, tzlp=tzlp, tzlm=tzlm, s=s_ref, diag=diag_ref, mxp=mxp, mxm=mxm, my=my,
        strips=strips, d_own=d_own, d_other=d_other, dx=dx, dy_hi=s_hi.at[3 * rows : 3 * rows + xdim, :],
        dy_lo=s_lo.at[3 * rows : 3 * rows + xdim, :], yb=yb, acc=acc, bx=bx,
    )
    finish(c, scaled, strip_q, r_ref, z_ref, send, w_ref, zown, sw, img_ref, ids, last)


def last_kernel(zdim, xdim, got, w_in, z_in, r_in, img_in, dir_in, sol_in, scal_ref, sol_ref, r_ref):
    peers = got.shape[0]
    _, sums = totals([got[p] for p in range(peers)])
    _, ratio, _, step = scalars(sums, scal_ref, False)

    def body(p, carry):
        image = w_in[p] + ratio * img_in[p][:xdim]
        r_ref[p] = r_in[p][:xdim] - step * image
        sol_ref[p] = sol_in[p] + step * (z_in[p] + ratio * dir_in[p])
        return carry

    lax.fori_loop(0, zdim, body, 0)


def call(kernel, name, args, outs, scratch=(), smem=0):
    specs = [pl.BlockSpec(memory_space=pltpu.SMEM)] * smem
    specs += [pl.BlockSpec(memory_space=pltpu.VMEM)] * (len(args) - smem)
    return pl.pallas_call(
        kernel,
        name=name,
        in_specs=specs,
        out_specs=[pl.BlockSpec(memory_space=pltpu.VMEM)] * len(outs),
        out_shape=[jax.ShapeDtypeStruct(o, jnp.float32) for o in outs],
        scratch_shapes=[pltpu.VMEM(s, jnp.float32) for s in scratch],
        compiler_params=pltpu.CompilerParams(vmem_limit_bytes=40 * 1024 * 1024),
    )(*args)


def local(right_side, permeability, storage, deflation, coarse_inverse, owners, margin):
    nx, ny, nz = (lax.axis_size(a) for a in ("gx", "gy", "gz"))
    vectors, zdim, xdim, ydim = deflation.shape
    order = coarse_inverse.shape[1]
    assert nz == 2 and ydim == LANES and 2 * zdim * STRIDE == LANES and vectors == 8
    gx, gy, gz = (lax.axis_index(a) for a in ("gx", "gy", "gz"))
    peers, planes, rows = nx * ny, 2 * zdim, xdim + 8
    me = gx * ny + gy
    off_x = jnp.array([0, 1, -1, 0, 0, 1, 1, -1, -1, 0], jnp.int32) + gx
    off_y = jnp.array([0, 0, 0, 1, -1, 1, -1, 1, -1, 0], jnp.int32) + gy
    there = (off_x >= 0) & (off_x < nx) & (off_y >= 0) & (off_y < ny)
    ids = jnp.where(there, off_x * ny + off_y, me)
    ids = jnp.where(jnp.arange(10) == 9, gz, ids)

    def swap(v):
        return lax.ppermute(v, "gz", [(0, 1), (1, 0)])

    def up(v, axis, count):
        return lax.ppermute(v, axis, [(i, i + 1) for i in range(count - 1)])

    def down(v, axis, count):
        return lax.ppermute(v, axis, [(i + 1, i) for i in range(count - 1)])

    fields = (permeability, storage, right_side)

    def edge_rows(lo, hi, at):
        parts = [v[:, lo:hi, :].reshape(-1, LANES) for v in fields]
        return jnp.concatenate(parts + [deflation[:, :, at, :].reshape(-1, LANES)], axis=0)

    x_lo = up(edge_rows(xdim - 3, xdim, xdim - 1), "gx", nx)
    x_hi = down(edge_rows(0, 3, 0), "gx", nx)
    others = [swap(v) for v in fields]
    d_other = swap(deflation)

    coeffs = jnp.sum(deflation * right_side[None], axis=(1, 2, 3))
    first_row = jnp.concatenate(
        [coeffs, owners.reshape(-1).astype(jnp.float32), margin.reshape(-1).astype(jnp.float32)]
    )
    first_row = jnp.pad(first_row, (0, LANES - first_row.shape[0]))
    table = lax.all_to_all(
        jnp.broadcast_to(first_row[None, None], (peers * nz, 1, LANES)),
        ("gx", "gy", "gz"), 0, 0, tiled=True,
    ).reshape(peers, nz, LANES)
    table = jnp.where(gz == 0, table, table[:, ::-1])
    hot = (ids[:5, None] == jnp.arange(peers)[None, :]).astype(jnp.float32)
    near = jnp.dot(hot, table.reshape(peers, nz * LANES), precision=PRECISE).reshape(5, nz, LANES)
    mt = near[:, :, 16:22].reshape(-1)
    near_owners = near[:, :, 8:16]
    wanted = jnp.concatenate(
        [near_owners[:3].transpose(1, 0, 2).reshape(-1), near_owners[3].reshape(-1), near_owners[4].reshape(-1)]
    )
    numbers = jnp.arange(order, dtype=jnp.float32)
    spare = PERIOD - 2 * vectors
    owner_all = jnp.pad(table[:, :, 8:16].reshape(peers, -1), ((0, 0), (0, spare)), constant_values=-1.0)
    known = jnp.pad(table[:, :, 0:8].reshape(peers, -1), ((0, 0), (0, spare))).reshape(-1, LANES)

    x_hi_other, x_lo_other = swap(x_hi), swap(x_lo)
    split = 3 * zdim * 3
    sides = [(v[:split], v[split:]) for v in (x_hi, x_lo, x_hi_other, x_lo_other)]
    strip_rows = 3 * rows + xdim
    main, strip_hi, strip_lo = call(
        lambda *refs: pack_kernel(zdim, xdim, *refs), "pack",
        [*fields, *others, *(v[0] for v in sides), deflation, d_other],
        [(3, planes, rows, LANES), (strip_rows, LANES), (strip_rows, LANES)],
    )
    dx = [v[1] for v in sides]
    s_lo = up(strip_hi, "gy", ny)
    s_hi = down(strip_lo, "gy", ny)
    whole = lax.all_gather(coarse_inverse, "gx", axis=0, tiled=True)
    select = jnp.dot((wanted[:, None] == numbers[None, :]).astype(jnp.float32), whole, precision=PRECISE)
    pick = (numbers[:, None] == owner_all.reshape(1, -1)).astype(jnp.float32)
    select = jnp.dot(select, pick, precision=PRECISE)

    tiles = known.shape[0]
    full, brick, one = (planes, rows, LANES), (planes, xdim, LANES), (rows, LANES)
    mine, slots = (zdim, xdim, LANES), (peers, SLOT, LANES)
    scratch = [full, full, (10 * vectors, LANES), (PERIOD, LANES), (2, zdim, LANES)]
    (send, w, z, sw, strips, *consts, rs) = call(
        lambda *refs: first_kernel(zdim, xdim, *refs), "first",
        [ids, mt, main, strip_hi, s_hi, s_lo, deflation, d_other, *dx, select, known],
        [slots, brick, mine, (xdim, LANES), (8, *one)] + [full] * 7 + [(2, *one)] * 3 + [one],
        scratch, smem=2,
    )
    state = [main]
    for iteration in range(ITERS - 1):
        first, last = iteration == 0, iteration == ITERS - 2
        got = lax.all_to_all(send, ("gx", "gy"), 0, 0, tiled=True)
        send, w, z, sw, rs, r, img, direct, sol, ist, known, kimg, scal = call(
            lambda *refs: next_kernel(zdim, xdim, first, last, *refs), f"step{iteration}",
            [ids, got, deflation, d_other, *dx, s_hi, s_lo, select, strips, *consts, known, w, z, sw, rs, *state],
            [(peers, 1, LANES) if last else slots, brick, mine, (xdim, LANES), one, full, full, mine, mine, one,
             (tiles, LANES), (tiles, LANES), (8, LANES)],
            scratch + [(planes, 8, LANES)], smem=1,
        )
        state = [r, img, direct, sol, ist, kimg, scal]
    got = lax.all_to_all(send, ("gx", "gy"), 0, 0, tiled=True)
    return tuple(call(
        lambda *refs: last_kernel(zdim, xdim, *refs), "last",
        [got, w, z, r, img, direct, sol, scal], [mine, mine],
    ))


def solution(mesh):
    in_specs = (
        P("gz", "gx", "gy"),
        P("gz", "gx", "gy"),
        P("gz", "gx", "gy"),
        P(None, "gz", "gx", "gy"),
        P("gx", None),
        P("gz", "gx", "gy", None),
        P("gz", "gx", "gy", None),
    )
    out_specs = (P("gz", "gx", "gy"), P("gz", "gx", "gy"))
    return jax.shard_map(local, mesh=mesh, in_specs=in_specs, out_specs=out_specs, check_vma=False)
```

```python
import jax
import jax.numpy as jnp
from jax import lax
from jax.experimental import pallas as pl
from jax.experimental.pallas import tpu as pltpu
from jax.sharding import PartitionSpec as P

ITERS = 4
RELAXATION = 0.7
PRECISE = lax.Precision.HIGHEST
LANES = 128
STRIDE = 8
PERIOD = 32


def conduct(first_perm, second_perm):
    return 2.0 * first_perm * second_perm / jnp.maximum(first_perm + second_perm, 0.05)


def turn(values, shift, axis):
    size = values.shape[axis]
    if isinstance(shift, int):
        shift = shift % size
        if shift == 0:
            return values
    return pltpu.roll(values, shift, axis)


def rem(a, b):
    return a % b if isinstance(a, int) else lax.rem(a, b)


def x_next(v):
    return turn(v, -1, 0)


def x_prev(v):
    return turn(v, 1, 0)


def y_next(v):
    return turn(v, -1, 1)


def y_prev(v):
    return turn(v, 1, 1)


def iota(shape, dim):
    return lax.broadcasted_iota(jnp.int32, shape, dim)


def place(shape):
    lane = iota(shape, 1)
    return lane >> 3, lane & 7


UNROLL = 8


def sweep(count, body, carry, unroll=None):
    unroll = min(count, unroll or UNROLL)
    if unroll == count:
        for i in range(count):
            carry = body(i, carry)
        return carry

    def several(i, carry):
        for u in range(unroll):
            carry = body(i * unroll + u, carry)
        return carry

    return lax.fori_loop(0, count // unroll, several, carry)


def eights(values):
    out = values[0:8]
    for t in range(1, values.shape[0] // 8):
        out = out + values[8 * t : 8 * t + 8]
    return out


def spread_row(acc_ref):
    count = acc_ref.shape[0]
    column = jnp.broadcast_to(jnp.sum(acc_ref[...], axis=1, keepdims=True), (count, LANES))
    match = iota((count, LANES), 0) == (iota((count, LANES), 1) & (count - 1))
    return jnp.sum(jnp.where(match, column, 0.0), axis=0, keepdims=True)


def prep_kernel(zdim, xdim, perm, stor, resid, d, owners, margin, row_ref, up_ref, down_ref, acc, line):
    for f, field in enumerate((perm, stor, resid)):
        for pz in range(zdim):
            at = (f * zdim + pz) * 3
            up_ref[at : at + 3, :] = field[pz, xdim - 3 : xdim, :]
            down_ref[at : at + 3, :] = field[pz, 0:3, :]
    vectors = d.shape[0]
    acc[...] = jnp.zeros(acc.shape, jnp.float32)
    for k in range(vectors):
        total = jnp.zeros((8, LANES), jnp.float32)
        for pz in range(zdim):
            at = (9 + k) * zdim + pz
            up_ref[at : at + 1, :] = d[k, pz, xdim - 1 : xdim, :]
            down_ref[at : at + 1, :] = d[k, pz, 0:1, :]
            total = total + eights(d[k, pz] * resid[pz])
        acc[k : k + 1, :] = jnp.sum(total, axis=0, keepdims=True)
    line[...] = jnp.zeros(line.shape, jnp.float32)
    line[0:1, 8 : 8 + vectors] = owners[...].astype(jnp.float32)
    line[0:1, 16:22] = margin[...].astype(jnp.float32)
    extra = line[0:1, :]
    extra = extra + turn(extra, PERIOD, 1)
    extra = extra + turn(extra, 2 * PERIOD, 1)
    row = spread_row(acc) + extra
    for p in range(row_ref.shape[0]):
        row_ref[p] = row


def coarse_kernel(ids, table, whole, select, known_ref, near, hot):
    order = whole.shape[0]
    zb = ids[9]
    place_of = (zb, 1 - zb)
    lane = iota((1, LANES), 1)
    lane8, sub8 = iota((8, LANES), 1), iota((8, LANES), 0)
    number = iota((8, order), 1).astype(jnp.float32)
    near[...] = jnp.zeros(near.shape, jnp.float32)
    for col in range(5):
        for b in range(2):
            row = table[2 * ids[col] + place_of[b]]
            near[2 * col + b : 2 * col + b + 1, :] = row
            owner = jnp.sum(jnp.where(lane8 == sub8 + 8, row, 0.0), axis=1, keepdims=True)
            at = 8 * (3 * b + col if col < 3 else 2 * col + b)
            hot[at : at + 8, :] = (number == owner).astype(jnp.float32)
    rows = jnp.dot(hot[...], whole[...], precision=PRECISE, preferred_element_type=jnp.float32)
    index = iota((order, LANES), 0).astype(jnp.float32)
    for t in range(known_ref.shape[0]):
        known = jnp.zeros((1, LANES), jnp.float32)
        owner = known - 1.0
        for i in range(4):
            for b in range(2):
                row = table[2 * (4 * t + i) + place_of[b]]
                mine = (lane >> 3) == 4 * i + b
                known = jnp.where(mine, turn(row, 8 * b, 1), known)
                owner = jnp.where(mine, turn(row, 8 * b - 8, 1), owner)
        known_ref[t : t + 1, :] = known
        pick = (index == owner).astype(jnp.float32)
        select[:, LANES * t : LANES * (t + 1)] = jnp.dot(
            rows, pick, precision=PRECISE, preferred_element_type=jnp.float32
        )


def pack_kernel(zdim, xdim, *refs):
    (own, other) = (refs[0:3], refs[3:6])
    (hi_own, lo_own, hi_other, lo_other, d_own, d_other) = refs[6:12]
    main, strip_hi, strip_lo = refs[12:15]
    rows = xdim + 8
    shape = (rows, LANES)
    plane_of, slot_of = place(shape)
    for f in range(3):
        acc = jnp.zeros(shape, jnp.float32)
        for p in range(2 * zdim):
            pz = p % zdim
            src = own if p < zdim else other
            hi = hi_own if p < zdim else hi_other
            lo = lo_own if p < zdim else lo_other
            at = (f * zdim + pz) * 3
            tile = jnp.concatenate(
                [hi[at : at + 3, :], jnp.zeros((2, LANES), jnp.float32), lo[at : at + 3, :]], axis=0
            )
            plane = jnp.concatenate([src[f][pz], tile], axis=0)
            main[f, p] = plane
            moved = turn(plane, STRIDE * p + 3, 1)
            acc = jnp.where((plane_of == p) & (slot_of < 6), moved, acc)
        strip_hi[f * rows : (f + 1) * rows, :] = acc
        strip_lo[f * rows : (f + 1) * rows, :] = acc
    lane = iota((xdim, LANES), 1)
    vectors = d_own.shape[0]
    hi_acc = jnp.zeros((xdim, LANES), jnp.float32)
    lo_acc = hi_acc
    for b, d_ref in ((0, d_own), (1, d_other)):
        for k in range(vectors):

            def body(pz, carry, k=k, b=b, d_ref=d_ref):
                one, two = carry
                at = STRIDE * (b * zdim + pz) + k
                moved = turn(d_ref[k, pz], at + 1, 1)
                one = jnp.where(lane == at, moved, one)
                two = jnp.where(lane == ((at + 1) & (LANES - 1)), moved, two)
                return one, two

            hi_acc, lo_acc = sweep(zdim, body, (hi_acc, lo_acc))
    strip_hi[3 * rows : 3 * rows + xdim, :] = hi_acc
    strip_lo[3 * rows : 3 * rows + xdim, :] = turn(lo_acc, -1, 1)


def solve_coarse(known, select_ref, yb_ref):
    total = 0.0
    for t, row in enumerate(known):
        total = total + select_ref[:, LANES * t : LANES * (t + 1)] * row
    column = jnp.sum(total, axis=1, keepdims=True)
    yb_ref[...] = jnp.broadcast_to(column, yb_ref.shape)


def finish(c, scaled, strip_q, r_ref, z_ref, send_ref, w_ref, zown_ref, sw_ref, img_ref, ids, last):
    zdim, xdim = c["d_own"].shape[1], c["d_own"].shape[2]
    planes, rows = 2 * zdim, xdim + 8
    vectors = c["d_own"].shape[0]
    strips = c["strips"]
    yb = c["yb"]
    plane_of, slot_of = place((rows, LANES))

    te, cxp, cxm, cin, cout, czp, czm, ss = (strips[i] for i in range(8))
    smooth = (
        cxp * x_next(strip_q)
        + cxm * x_prev(strip_q)
        + cin * turn(strip_q, 4, 1)
        + cout * turn(strip_q, 2, 1)
        + czp * turn(strip_q, -STRIDE, 1)
        + czm * turn(strip_q, STRIDE, 1)
    )
    strip_z = (2.0 - RELAXATION) * strip_q + ss * smooth
    lane16 = iota((2 * vectors, LANES), 1)
    row16 = iota((2 * vectors, LANES), 0)
    wanted = row16 == (lane16 >> 6) * vectors + (lane16 & 7)
    for side, d_strip in ((0, c["dy_hi"]), (1, c["dy_lo"])):
        at = 6 * vectors + side * 2 * vectors
        coeff = jnp.sum(jnp.where(wanted, yb[at : at + 2 * vectors, :], 0.0), axis=0, keepdims=True)
        t = d_strip[...] * coeff
        t = t + turn(t, -1, 1)
        t = t + turn(t, -2, 1)
        t = t + turn(t, -4, 1)
        t = jnp.where(slot_of[:xdim] == 5 + side, turn(t, 5 + side, 1), 0.0)
        t = jnp.concatenate([t, jnp.zeros((8, LANES), jnp.float32)], axis=0)
        strip_z = strip_z + t
    edge_q = te * strip_q
    edge_z = te * strip_z

    row8 = iota((8, LANES), 0)
    for b in range(2):
        d_ref = c["d_own"] if b == 0 else c["d_other"]
        x_rows = []
        for side in range(2):
            dx = c["dx"][2 * b + side]
            acc = 0.0
            for k in range(vectors):
                at = (3 * b + 1 + side) * vectors + k
                start = (9 + k) * zdim
                acc = acc + dx[start : start + zdim, :] * yb[at : at + 1, :]
            x_rows.append(acc)
        c["bx"][0] = x_rows[0]
        c["bx"][1] = x_rows[1]
        mxp, mxm, my = c["mxp"][b], c["mxm"][b], c["my"][b]

        def body(pz, carry, b=b, d_ref=d_ref, mxp=mxp, mxm=mxm, my=my):
            p = b * zdim + pz
            q = scaled[p]
            tx, ty = c["tx"][p], c["ty"][p]
            acc = tx * mxp * x_next(q) + mxm * x_prev(tx * q)
            acc = acc + ty * y_next(q) + y_prev(ty * q)
            acc = acc + my * turn(edge_q, LANES - 6 - STRIDE * p, 1)
            acc = acc + c["tzlp"][p] * scaled[rem(p + 1, planes)]
            acc = acc + c["tzlm"][p] * scaled[rem(p + planes - 1, planes)]
            z = (2.0 - RELAXATION) * q + c["s"][p] * acc
            field = 0.0
            for k in range(vectors):
                at = 3 * b * vectors + k
                field = field + d_ref[k, pz] * yb[at : at + 1, :]
            tile = jnp.where(row8 == 0, c["bx"][0, pl.ds(pz, 1), :], 0.0)
            tile = jnp.where(row8 == 7, c["bx"][1, pl.ds(pz, 1), :], tile)
            z = z + jnp.concatenate([field, tile], axis=0)
            z_ref[p] = z
            if b == 0:
                zown_ref[pz] = z[:xdim]
            return carry

        sweep(zdim, body, 0)

    lane = iota((rows, LANES), 1)
    edge = jnp.where((lane == 0) | (lane == LANES - 1), 1.0, 0.0)
    plane64, slot64 = plane_of[:xdim], slot_of[:xdim]
    zero = jnp.zeros((8, LANES), jnp.float32)
    scal = (zero, zero, zero)
    coeffs = []
    packed = jnp.zeros((xdim, LANES), jnp.float32)
    for b in range(2):
        d_ref = c["d_own"] if b == 0 else c["d_other"]

        def body(pz, carry, b=b, d_ref=d_ref):
            scal, sums, packed = carry
            p = b * zdim + pz
            z = z_ref[p]
            tx, ty = c["tx"][p], c["ty"][p]
            before = rem(p + planes - 1, planes)
            acc = tx * x_next(z) + x_prev(tx * z)
            acc = acc + ty * y_next(z) + y_prev(ty * z)
            acc = acc + edge * turn(edge_z, LANES - 6 - STRIDE * p, 1)
            acc = acc + c["tz"][p] * z_ref[rem(p + 1, planes)]
            acc = acc + c["tz"][before] * z_ref[before]
            w = (c["diag"][p] * z - acc)[:xdim]
            z = z[:xdim]
            w_ref[p] = w
            rz, zw, zi = scal
            rz = rz + eights(r_ref[p][:xdim] * z)
            zw = zw + eights(w * z)
            if img_ref is not None:
                zi = zi + eights(img_ref[p][:xdim] * z)
            sums = tuple(sums[k] + eights(d_ref[k, pz] * w) for k in range(vectors))
            moved = turn(w, rem(STRIDE * p + 2, LANES), 1)
            packed = jnp.where((plane64 == p) & (slot64 < 4), moved, packed)
            return (rz, zw, zi), sums, packed

        scal, sums, packed = sweep(zdim, body, (scal, (zero,) * vectors, packed))
        coeffs.extend(sums)

    acc_ref = c["acc"]
    acc_ref[...] = jnp.zeros(acc_ref.shape, jnp.float32)
    for j, value in enumerate(coeffs + list(scal)):
        acc_ref[j : j + 1, :] = jnp.sum(value, axis=0, keepdims=True)
    row = spread_row(acc_ref)
    peers = send_ref.shape[0]
    if last:
        for p in range(peers):
            send_ref[p] = row
        return
    for p in range(peers):
        send_ref[p, planes, 0:1, :] = row
    sw_ref[...] = packed
    for p in range(planes):
        send_ref[ids[1], p] = w_ref[p, xdim - 2 : xdim, :]
        send_ref[ids[2], p] = w_ref[p, 0:2, :]
    part = xdim // 4
    pair = (iota((part, LANES), 1) & 7) >> 1
    to_hi = jnp.zeros((part, LANES), jnp.float32)
    to_lo = to_hi
    for g in range(4):
        rows_g = packed[g * part : (g + 1) * part]
        to_hi = jnp.where(pair == g, turn(rows_g, 2 * g, 1), to_hi)
        to_lo = jnp.where(pair == g, turn(rows_g, 2 * g - 2, 1), to_lo)
    for i in range(part // 2):
        send_ref[ids[3], i] = to_hi[2 * i : 2 * i + 2]
        send_ref[ids[4], i] = to_lo[2 * i : 2 * i + 2]
    for i in (5, 6):
        send_ref[ids[i], 0, 0:1, :] = packed[xdim - 1 : xdim, :]
    for i in (7, 8):
        send_ref[ids[i], 0, 0:1, :] = packed[0:1, :]


def first_kernel(zdim, xdim, *refs):
    (ids, near, f, s_own, s_hi, s_lo, d_own, d_other) = refs[0:8]
    dx = refs[8:12]
    (select, known_ref) = refs[12:14]
    (send, w_ref, zown, sw, strips, tx, ty, tz, tzlp, tzlm, s_ref, diag_ref, mxp, mxm, my, rs_ref) = refs[14:30]
    (scaled, z_ref, yb, acc, bx) = refs[30:35]
    planes, rows = 2 * zdim, xdim + 8
    shape = (rows, LANES)
    row, lane = iota(shape, 0), iota(shape, 1)
    plane_of, slot_of = place(shape)
    zb = ids[9]
    cut = jnp.where(zb == 0, planes - 1, zdim - 1)

    def mg(col, b, d):
        at = 2 * col + b
        return near[at : at + 1, 16 + d : 17 + d]

    def by_row(b, d):
        return jnp.where(row < xdim, mg(0, b, d), jnp.where(row < xdim + 4, mg(1, b, d), mg(2, b, d)))

    for b in range(2):
        mxp[b] = jnp.where(row == xdim - 1, mg(0, b, 3), jnp.where(row == rows - 1, mg(2, b, 3), 1.0))
        mxm[b] = jnp.where(row == 0, mg(0, b, 2), jnp.where(row == xdim, mg(1, b, 2), 1.0))
        my[b] = jnp.where(lane == LANES - 1, by_row(b, 5), jnp.where(lane == 0, by_row(b, 4), 0.0))

    def strip(i):
        at = slice(i * rows, (i + 1) * rows)
        own, hi, lo = s_own[at, :], s_hi[at, :], s_lo[at, :]
        out = jnp.where((slot_of == 1) | (slot_of == 2), turn(own, -1, 1), 0.0)
        out = jnp.where(slot_of == 5, turn(hi, 2, 1), out)
        out = jnp.where(slot_of == 3, turn(hi, -1, 1), out)
        out = jnp.where(slot_of == 0, turn(hi, -5, 1), out)
        out = jnp.where(slot_of == 6, turn(lo, 4, 1), out)
        out = jnp.where(slot_of == 4, turn(lo, 3, 1), out)
        return jnp.where(slot_of == 7, turn(lo, 7, 1), out)

    ps, st, rs = strip(0), strip(1), strip(2)
    rs_ref[...] = rs
    face = (slot_of == 5) | (slot_of == 6)
    t_x = conduct(ps, x_next(ps))
    t_z = jnp.where(plane_of == cut, 0.0, conduct(ps, turn(ps, -STRIDE, 1)))
    t_in = jnp.where(face, conduct(ps, turn(ps, 4, 1)), 0.0)
    t_out = jnp.where(face, conduct(ps, turn(ps, 2, 1)), 0.0)
    t_far = jnp.where(
        slot_of == 3,
        conduct(ps, turn(ps, 3, 1)),
        jnp.where(slot_of == 4, conduct(ps, turn(ps, -3, 1)), 0.0),
    )
    diag_s = st + t_x + x_prev(t_x) + t_z + turn(t_z, STRIDE, 1)
    diag_s = diag_s + t_in + t_out + turn(t_out, -2, 1) + t_far
    ss = jnp.where(diag_s > 0.0, RELAXATION / jnp.where(diag_s > 0.0, diag_s, 1.0), 0.0)

    def by_side(b, d_hi, d_lo):
        return jnp.where(slot_of == 5, mg(3, b, d_hi), mg(4, b, d_lo))

    def by_brick(d_hi, d_lo):
        return jnp.where(plane_of < zdim, by_side(0, d_hi, d_lo), by_side(1, d_hi, d_lo))

    def only(values):
        return jnp.where(face, values, 0.0)

    strips[0] = t_in
    strips[1] = only(t_x * jnp.where(row == xdim - 1, by_brick(3, 3), 1.0))
    strips[2] = only(x_prev(t_x) * jnp.where(row == 0, by_brick(2, 2), 1.0))
    strips[3] = t_in * by_brick(4, 5)
    strips[4] = t_out
    high = (plane_of == zdim - 1) | (plane_of == planes - 1)
    low = (plane_of == 0) | (plane_of == zdim)
    strips[5] = only(t_z * jnp.where(high, by_brick(1, 1), 1.0))
    strips[6] = only(turn(t_z, STRIDE, 1) * jnp.where(low, by_brick(0, 0), 1.0))

    inside = lane < LANES - 1

    def transmit(p, carry):
        here = f[0, p]
        after = f[0, rem(p + 1, planes)]
        tx[p] = conduct(here, x_next(here))
        ty[p] = jnp.where(inside, conduct(here, y_next(here)), 0.0)
        tz[p] = conduct(here, after) * jnp.where(p == cut, 0.0, 1.0)
        return carry

    sweep(planes, transmit, 0)
    edge = (lane == 0) | (lane == LANES - 1)
    inner = jnp.zeros(shape, jnp.float32)
    for b in range(2):
        m_hi, m_lo = by_row(b, 1), by_row(b, 0)

        def diagonal(pz, inner, b=b, m_hi=m_hi, m_lo=m_lo):
            p = b * zdim + pz
            t_x, t_y, t_z = tx[p], ty[p], tz[p]
            t_b = tz[rem(p + planes - 1, planes)]
            total = f[1, p] + t_x + x_prev(t_x) + t_y + y_prev(t_y) + t_z + t_b
            total = total + jnp.where(edge, turn(t_in, LANES - 6 - STRIDE * p, 1), 0.0)
            relax = jnp.where(total > 0.0, RELAXATION / jnp.where(total > 0.0, total, 1.0), 0.0)
            diag_ref[p] = total
            s_ref[p] = relax
            tzlp[p] = t_z * jnp.where(pz == zdim - 1, m_hi, 1.0)
            tzlm[p] = t_b * jnp.where(pz == 0, m_lo, 1.0)
            scaled[p] = relax * f[2, p]
            moved = turn(relax, rem(STRIDE * p + 2, LANES), 1)
            return jnp.where((plane_of == p) & ((slot_of == 1) | (slot_of == 2)), moved, inner)

        inner = sweep(zdim, diagonal, inner)
    ss = jnp.where((slot_of == 1) | (slot_of == 2), inner, ss)
    strips[7] = ss

    known = [known_ref[t : t + 1, :] for t in range(known_ref.shape[0])]
    solve_coarse(known, select, yb)
    c = dict(
        tx=tx, ty=ty, tz=tz, tzlp=tzlp, tzlm=tzlm, s=s_ref, diag=diag_ref, mxp=mxp, mxm=mxm, my=my,
        strips=strips, d_own=d_own, d_other=d_other, dx=dx, dy_hi=s_hi.at[3 * rows : 3 * rows + xdim, :],
        dy_lo=s_lo.at[3 * rows : 3 * rows + xdim, :], yb=yb, acc=acc, bx=bx,
    )
    finish(c, scaled, ss * rs, f.at[2], z_ref, send, w_ref, zown, sw, None, ids, False)


def totals(rows):
    lane = iota((1, LANES), 1)
    group = lane >> 5
    tiles = []
    for t in range(len(rows) // 4):
        tile = 0.0
        for i in range(4):
            tile = tile + jnp.where(group == i, rows[4 * t + i], 0.0)
        tiles.append(tile)
    total = tiles[0]
    for tile in tiles[1:]:
        total = total + tile
    index = lane & (PERIOD - 1)
    sums = [
        jnp.sum(jnp.where(index == 16 + j, total, 0.0), axis=1, keepdims=True) for j in range(3)
    ]
    return tiles, sums


def scalars(sums, scal_ref, first):
    inner = sums[0]
    if first:
        ratio = jnp.zeros_like(inner)
        curvature = sums[1]
    else:
        ratio = inner / scal_ref[0:1, 0:1]
        curvature = sums[1] + ratio * (2.0 * sums[2] + ratio * scal_ref[1:2, 0:1])
    return inner, ratio, curvature, inner / curvature


def next_kernel(zdim, xdim, first, last, *refs):
    refs = list(refs)

    def take(n):
        out, refs[:n] = refs[:n], []
        return out

    ids, got, d_own, d_other, *dx = take(8)
    s_hi, s_lo, select, strips, tx, ty, tz, tzlp, tzlm, s_ref, diag_ref, mxp, mxm, my = take(14)
    known_ref, w_in, z_in, sw_in, rs_in = take(5)
    if first:
        (f,) = take(1)
        r_in = f.at[2]
    else:
        r_in, img_in, dir_in, sol_in, is_in, kimg_ref, scal_ref = take(7)
    send, w_ref, zown, sw, rs_ref, r_ref, img_ref, dir_ref, sol_ref, is_ref, known_out, kimg_out, scal_out = take(13)
    scaled, z_ref, yb, acc, bx, tiles_ref = take(6)
    planes, rows = 2 * zdim, xdim + 8
    plane_of, slot_of = place((rows, LANES))

    peers = got.shape[0]
    tiles, sums = totals([got[p, planes, 0:1, :] for p in range(peers)])
    inner, ratio, curvature, step = scalars(sums, None if first else scal_ref, first)
    scal_out[0:1, :] = jnp.broadcast_to(inner, (1, LANES))
    scal_out[1:2, :] = jnp.broadcast_to(curvature, (1, LANES))
    known = []
    for t, tile in enumerate(tiles):
        if not first:
            tile = tile + ratio * kimg_ref[t : t + 1, :]
        kimg_out[t : t + 1, :] = tile
        value = known_ref[t : t + 1, :] - step * tile
        known_out[t : t + 1, :] = value
        known.append(value)
    solve_coarse(known, select, yb)

    part = xdim // 4
    for i in range(part // 2):
        tiles_ref[0, 2 * i : 2 * i + 2, :] = got[ids[3], i]
        tiles_ref[1, 2 * i : 2 * i + 2, :] = got[ids[4], i]
    from_hi, from_lo = tiles_ref[0], tiles_ref[1]
    own = sw_in[...]
    slot_part = slot_of[:part]
    blocks = []
    for g in range(4):
        value = own[g * part : (g + 1) * part]
        value = jnp.where(slot_part == 5, turn(from_hi, 5 - 2 * g, 1), value)
        value = jnp.where(slot_part == 3, turn(from_hi, 2 - 2 * g, 1), value)
        value = jnp.where(slot_part == 4, turn(from_lo, 4 - 2 * g, 1), value)
        value = jnp.where(slot_part == 6, turn(from_lo, 5 - 2 * g, 1), value)
        blocks.append(value)
    slot8, row8 = slot_of[:8], iota((8, LANES), 0)
    tile = jnp.zeros((8, LANES), jnp.float32)
    for i, at, want, shift in ((5, 0, 5, 3), (6, 0, 6, 5), (7, 7, 5, 3), (8, 7, 6, 5)):
        value = turn(jnp.broadcast_to(got[ids[i], 0, 0:1, :], (8, LANES)), shift, 1)
        tile = jnp.where((row8 == at) & (slot8 == want), value, tile)
    ws = jnp.concatenate(blocks + [tile], axis=0)
    ws = jnp.where((slot_of == 0) | (slot_of == 7), 0.0, ws)
    if not first:
        ws = ws + ratio * is_in[...]
    is_ref[...] = ws
    rs = rs_in[...] - step * ws
    rs_ref[...] = rs
    strip_q = strips[7] * rs

    tiles_ref[...] = jnp.zeros(tiles_ref.shape, jnp.float32)
    for p in range(planes):
        tiles_ref[p, 0:2, :] = got[ids[1], p]
        tiles_ref[p, 6:8, :] = got[ids[2], p]

    def update(p, carry):
        image = jnp.concatenate([w_in[p], tiles_ref[p, 0:8, :]], axis=0)
        if not first:
            image = image + ratio * img_in[p]
        img_ref[p] = image
        r = r_in[p] - step * image
        r_ref[p] = r
        scaled[p] = s_ref[p] * r
        return carry

    sweep(planes, update, 0)

    def advance(p, carry):
        d = z_in[p]
        if first:
            sol_ref[p] = step * d
        else:
            d = d + ratio * dir_in[p]
            sol_ref[p] = sol_in[p] + step * d
        dir_ref[p] = d
        return carry

    sweep(zdim, advance, 0)
    c = dict(
        tx=tx, ty=ty, tz=tz, tzlp=tzlp, tzlm=tzlm, s=s_ref, diag=diag_ref, mxp=mxp, mxm=mxm, my=my,
        strips=strips, d_own=d_own, d_other=d_other, dx=dx, dy_hi=s_hi.at[3 * rows : 3 * rows + xdim, :],
        dy_lo=s_lo.at[3 * rows : 3 * rows + xdim, :], yb=yb, acc=acc, bx=bx,
    )
    finish(c, scaled, strip_q, r_ref, z_ref, send, w_ref, zown, sw, img_ref, ids, last)


def last_kernel(zdim, xdim, got, w_in, z_in, r_in, img_in, dir_in, sol_in, scal_ref, sol_ref, r_ref):
    peers = got.shape[0]
    _, sums = totals([got[p] for p in range(peers)])
    sums = [0.5 * value for value in sums]
    _, ratio, _, step = scalars(sums, scal_ref, False)

    def body(p, carry):
        image = w_in[p] + ratio * img_in[p][:xdim]
        r_ref[p] = r_in[p][:xdim] - step * image
        sol_ref[p] = sol_in[p] + step * (z_in[p] + ratio * dir_in[p])
        return carry

    sweep(zdim, body, 0)


def call(kernel, name, args, outs, scratch=(), smem=0):
    specs = [pl.BlockSpec(memory_space=pltpu.SMEM)] * smem
    specs += [pl.BlockSpec(memory_space=pltpu.VMEM)] * (len(args) - smem)
    return pl.pallas_call(
        kernel,
        name=name,
        in_specs=specs,
        out_specs=[pl.BlockSpec(memory_space=pltpu.VMEM)] * len(outs),
        out_shape=[jax.ShapeDtypeStruct(o, jnp.float32) for o in outs],
        scratch_shapes=[pltpu.VMEM(s, jnp.float32) for s in scratch],
        compiler_params=pltpu.CompilerParams(vmem_limit_bytes=40 * 1024 * 1024),
    )(*args)


def local(right_side, permeability, storage, deflation, coarse_inverse, owners, margin):
    nx, ny, nz = (lax.axis_size(a) for a in ("gx", "gy", "gz"))
    vectors, zdim, xdim, ydim = deflation.shape
    order = coarse_inverse.shape[1]
    assert nz == 2 and ydim == LANES and 2 * zdim * STRIDE == LANES and vectors == 8
    gx, gy, gz = (lax.axis_index(a) for a in ("gx", "gy", "gz"))
    peers, planes, rows = nx * ny, 2 * zdim, xdim + 8
    me = gx * ny + gy
    off_x = jnp.array([0, 1, -1, 0, 0, 1, 1, -1, -1, 0], jnp.int32) + gx
    off_y = jnp.array([0, 0, 0, 1, -1, 1, -1, 1, -1, 0], jnp.int32) + gy
    there = (off_x >= 0) & (off_x < nx) & (off_y >= 0) & (off_y < ny)
    ids = jnp.where(there, off_x * ny + off_y, me)
    ids = jnp.where(jnp.arange(10) == 9, gz, ids)

    def swap(v):
        return lax.ppermute(v, "gz", [(0, 1), (1, 0)])

    def up(v, axis, count):
        return lax.ppermute(v, axis, [(i, i + 1) for i in range(count - 1)])

    def down(v, axis, count):
        return lax.ppermute(v, axis, [(i + 1, i) for i in range(count - 1)])

    fields = (permeability, storage, right_side)
    others = [swap(v) for v in fields]
    d_other = swap(deflation)
    edge_rows = ((9 + vectors) * zdim, LANES)
    first_row, x_up, x_down = call(
        lambda *refs: prep_kernel(zdim, xdim, *refs), "prep",
        [*fields, deflation, owners.reshape(1, -1), margin.reshape(1, -1)],
        [(peers * nz, 1, LANES), edge_rows, edge_rows],
        [(PERIOD, LANES), (8, LANES)],
    )
    x_lo, x_hi = up(x_up, "gx", nx), down(x_down, "gx", nx)
    table = lax.all_to_all(first_row, ("gx", "gy", "gz"), 0, 0, tiled=True)
    dx = [x_hi, x_lo, swap(x_hi), swap(x_lo)]
    strip_rows = 3 * rows + xdim
    main, strip_hi, strip_lo = call(
        lambda *refs: pack_kernel(zdim, xdim, *refs), "pack",
        [*fields, *others, *dx, deflation, d_other],
        [(3, planes, rows, LANES), (strip_rows, LANES), (strip_rows, LANES)],
    )
    s_lo = up(strip_hi, "gy", ny)
    s_hi = down(strip_lo, "gy", ny)
    coarse_inverse, _ = lax.optimization_barrier((coarse_inverse, strip_hi))
    whole = lax.all_gather(coarse_inverse, "gx", axis=0, tiled=True)
    tiles = peers * PERIOD // LANES
    select, known, near = call(
        coarse_kernel, "coarse", [ids, table, whole],
        [(10 * vectors, peers * PERIOD), (tiles, LANES), (16, LANES)],
        [(10 * vectors, order)], smem=1,
    )
    full, brick, one = (planes, rows, LANES), (planes, xdim, LANES), (rows, LANES)
    mine, slots = (zdim, xdim, LANES), (peers, planes + 1, 2, LANES)
    scratch = [full, full, (10 * vectors, LANES), (PERIOD, LANES), (2, zdim, LANES)]
    (send, w, z, sw, strips, *consts, rs) = call(
        lambda *refs: first_kernel(zdim, xdim, *refs), "first",
        [ids, near, main, strip_hi, s_hi, s_lo, deflation, d_other, *dx, select, known],
        [slots, brick, mine, (xdim, LANES), (8, *one)] + [full] * 7 + [(2, *one)] * 3 + [one],
        scratch, smem=1,
    )
    state = [main]
    for iteration in range(ITERS - 1):
        first, last = iteration == 0, iteration == ITERS - 2
        got = lax.all_to_all(send, ("gx", "gy"), 0, 0, tiled=True)
        send, w, z, sw, rs, r, img, direct, sol, ist, known, kimg, scal = call(
            lambda *refs: next_kernel(zdim, xdim, first, last, *refs), f"step{iteration}",
            [ids, got, deflation, d_other, *dx, s_hi, s_lo, select, strips, *consts, known, w, z, sw, rs, *state],
            [(peers * nz, 1, LANES) if last else slots, brick, mine, (xdim, LANES), one, full, full, mine, mine, one,
             (tiles, LANES), (tiles, LANES), (8, LANES)],
            scratch + [(planes, max(8, xdim // 4), LANES)], smem=1,
        )
        state = [r, img, direct, sol, ist, kimg, scal]
    got = lax.all_to_all(send, ("gx", "gy", "gz"), 0, 0, tiled=True)
    return tuple(call(
        lambda *refs: last_kernel(zdim, xdim, *refs), "last",
        [got, w, z, r, img, direct, sol, scal], [mine, mine],
    ))


def solution(mesh):
    in_specs = (
        P("gz", "gx", "gy"),
        P("gz", "gx", "gy"),
        P("gz", "gx", "gy"),
        P(None, "gz", "gx", "gy"),
        P("gx", None),
        P("gz", "gx", "gy", None),
        P("gz", "gx", "gy", None),
    )
    out_specs = (P("gz", "gx", "gy"), P("gz", "gx", "gy"))
    return jax.shard_map(local, mesh=mesh, in_specs=in_specs, out_specs=out_specs, check_vma=False)
```

```python
import jax
import jax.numpy as jnp
from jax import lax
from jax.experimental import pallas as pl
from jax.experimental.pallas import tpu as pltpu
from jax.sharding import PartitionSpec as P

ITERS = 4
RELAXATION = 0.7
PRECISE = lax.Precision.HIGHEST
LANES = 128
STRIDE = 8
PERIOD = 32


def conduct(first_perm, second_perm):
    return 2.0 * first_perm * second_perm / jnp.maximum(first_perm + second_perm, 0.05)


def turn(values, shift, axis):
    size = values.shape[axis]
    if isinstance(shift, int):
        shift = shift % size
        if shift == 0:
            return values
    return pltpu.roll(values, shift, axis)


def rem(a, b):
    return a % b if isinstance(a, int) else lax.rem(a, b)


def x_next(v):
    return turn(v, -1, 0)


def x_prev(v):
    return turn(v, 1, 0)


def y_next(v):
    return turn(v, -1, 1)


def y_prev(v):
    return turn(v, 1, 1)


def iota(shape, dim):
    return lax.broadcasted_iota(jnp.int32, shape, dim)


def place(shape):
    lane = iota(shape, 1)
    return lane >> 3, lane & 7


def mirror(p, zdim):
    return p + lax.axis_index("gz") * (zdim - 1 - 2 * p)


def by_tiles(mask, values, tiles):
    parts, at = [], 0
    for t in tiles:
        if 8 * t > at:
            parts.append(values[at : 8 * t])
        at = 8 * (t + 1)
        parts.append(mask[8 * t : at] * values[8 * t : at])
    if at < values.shape[0]:
        parts.append(values[at:])
    return jnp.concatenate(parts, axis=0)


def eights(values):
    out = values[0:8]
    for t in range(1, values.shape[0] // 8):
        out = out + values[8 * t : 8 * t + 8]
    return out


def spread_row(acc_ref):
    count = acc_ref.shape[0]
    column = jnp.broadcast_to(jnp.sum(acc_ref[...], axis=1, keepdims=True), (count, LANES))
    match = iota((count, LANES), 0) == (iota((count, LANES), 1) & (count - 1))
    return jnp.sum(jnp.where(match, column, 0.0), axis=0, keepdims=True)


def prep_kernel(zdim, xdim, perm, stor, resid, d, whose, row_ref, up_ref, down_ref, acc, line):
    for f, field in enumerate((perm, stor, resid)):
        for pz in range(zdim):
            at = (f * zdim + pz) * 3
            up_ref[at : at + 3, :] = field[mirror(pz, zdim), xdim - 3 : xdim, :]
            down_ref[at : at + 3, :] = field[mirror(pz, zdim), 0:3, :]
    vectors = d.shape[0]
    acc[...] = jnp.zeros(acc.shape, jnp.float32)
    for k in range(vectors):
        total = jnp.zeros((8, LANES), jnp.float32)
        for pz in range(zdim):
            at = (9 + k) * zdim + pz
            up_ref[at : at + 1, :] = d[k, mirror(pz, zdim), xdim - 1 : xdim, :]
            down_ref[at : at + 1, :] = d[k, mirror(pz, zdim), 0:1, :]
            total = total + eights(d[k, pz] * resid[pz])
        acc[k : k + 1, :] = jnp.sum(total, axis=0, keepdims=True)
    line[...] = jnp.zeros(line.shape, jnp.float32)
    line[0:1, 8 : 8 + vectors] = whose[:, :vectors].astype(jnp.float32)
    line[0:1, 16:22] = whose[:, vectors:].astype(jnp.float32)
    extra = line[0:1, :]
    extra = extra + turn(extra, PERIOD, 1)
    extra = extra + turn(extra, 2 * PERIOD, 1)
    row = spread_row(acc) + extra
    for p in range(row_ref.shape[0]):
        row_ref[p] = row


def coarse_kernel(ids, table, whole, select, known_ref, near, hot):
    order = whole.shape[0]
    zb = ids[9]
    place_of = (zb, 1 - zb)
    lane = iota((1, LANES), 1)
    lane8, sub8 = iota((8, LANES), 1), iota((8, LANES), 0)
    number = iota((8, order), 1).astype(jnp.float32)
    near[...] = jnp.zeros(near.shape, jnp.float32)
    for col in range(5):
        for b in range(2):
            row = table[2 * ids[col] + place_of[b]]
            near[2 * col + b : 2 * col + b + 1, :] = row
            owner = jnp.sum(jnp.where(lane8 == sub8 + 8, row, 0.0), axis=1, keepdims=True)
            at = 8 * (3 * b + col if col < 3 else 2 * col + b)
            hot[at : at + 8, :] = (number == owner).astype(jnp.float32)
    rows = jnp.dot(hot[...], whole[...], precision=PRECISE, preferred_element_type=jnp.float32)
    index = iota((order, LANES), 0).astype(jnp.float32)
    for t in range(known_ref.shape[0]):
        known = jnp.zeros((1, LANES), jnp.float32)
        owner = known - 1.0
        for i in range(4):
            for b in range(2):
                row = table[2 * (4 * t + i) + place_of[b]]
                mine = (lane >> 3) == 4 * i + b
                known = jnp.where(mine, turn(row, 8 * b, 1), known)
                owner = jnp.where(mine, turn(row, 8 * b - 8, 1), owner)
        known_ref[t : t + 1, :] = known
        pick = (index == owner).astype(jnp.float32)
        select[:, LANES * t : LANES * (t + 1)] = jnp.dot(
            rows, pick, precision=PRECISE, preferred_element_type=jnp.float32
        )


def plane_of_field(fields, halos, f, p):
    own, other = fields
    zdim, xdim = own[0].shape[0], own[0].shape[1]
    hi_own, lo_own, hi_other, lo_other = halos
    src, hi, lo = (own, hi_own, lo_own) if p < zdim else (other, hi_other, lo_other)
    at = (f * zdim + (p if p < zdim else 2 * zdim - 1 - p)) * 3
    gap = jnp.zeros((2, LANES), jnp.float32)
    tile = jnp.concatenate([hi[at : at + 3, :], gap, lo[at : at + 3, :]], axis=0)
    return jnp.concatenate([src[f][mirror(p % zdim, zdim)], tile], axis=0)


def pack_kernel(zdim, xdim, *refs):
    fields = (refs[0:3], refs[3:6])
    halos, d_own = refs[6:10], refs[10]
    strip_hi, strip_lo = refs[11:13]
    rows = xdim + 8
    shape = (rows, LANES)
    plane_of, slot_of = place(shape)
    for f in range(3):
        acc = jnp.zeros(shape, jnp.float32)
        for p in range(zdim + 3):
            moved = turn(plane_of_field(fields, halos, f, p), STRIDE * p + 3, 1)
            acc = jnp.where((plane_of == p) & (slot_of < 6), moved, acc)
        strip_hi[f * rows : (f + 1) * rows, :] = acc
        strip_lo[f * rows : (f + 1) * rows, :] = acc
    lane = iota((xdim, LANES), 1)
    vectors = d_own.shape[0]
    hi_acc = jnp.zeros((xdim, LANES), jnp.float32)
    lo_acc = hi_acc
    for k in range(vectors):
        for p in range(zdim):
            at = STRIDE * p + k
            moved = turn(d_own[k, mirror(p, zdim)], at + 1, 1)
            hi_acc = jnp.where(lane == at, moved, hi_acc)
            lo_acc = jnp.where(lane == at + 1, moved, lo_acc)
    strip_hi[3 * rows : 3 * rows + xdim, :] = hi_acc
    strip_lo[3 * rows : 3 * rows + xdim, :] = turn(lo_acc, -1, 1)


def solve_coarse(known, select_ref, yb_ref):
    total = 0.0
    for t, row in enumerate(known):
        total = total + select_ref[:, LANES * t : LANES * (t + 1)] * row
    column = jnp.sum(total, axis=1, keepdims=True)
    yb_ref[...] = jnp.broadcast_to(column, yb_ref.shape)


def finish(c, scaled, strip_q, r_ref, z_ref, send_ref, w_ref, zown_ref, sw_ref, zsend_ref, img_ref, ids, last):
    zdim, xdim = c["d_own"].shape[1], c["d_own"].shape[2]
    rows = xdim + 8
    vectors = c["d_own"].shape[0]
    strips = c["strips"]
    yb = c["yb"]
    plane_of, slot_of = place((rows, LANES))

    te, cxp, cxm, cin, cout, czp, czm, ss = (strips[i] for i in range(8))
    smooth = (
        cxp * x_next(strip_q)
        + cxm * x_prev(strip_q)
        + cin * turn(strip_q, 4, 1)
        + cout * turn(strip_q, 2, 1)
        + czp * turn(strip_q, -STRIDE, 1)
        + czm * turn(strip_q, STRIDE, 1)
    )
    strip_z = (2.0 - RELAXATION) * strip_q + ss * smooth
    lane8, row8 = iota((vectors, LANES), 1), iota((vectors, LANES), 0)
    wanted = row8 == (lane8 & 7)
    for side, d_strip in ((0, c["dy_hi"]), (1, c["dy_lo"])):
        at = 6 * vectors + side * 2 * vectors
        coeff = jnp.sum(jnp.where(wanted, yb[at : at + vectors, :], 0.0), axis=0, keepdims=True)
        t = d_strip[...] * coeff
        t = t + turn(t, -1, 1)
        t = t + turn(t, -2, 1)
        t = t + turn(t, -4, 1)
        t = jnp.where(slot_of[:xdim] == 5 + side, turn(t, 5 + side, 1), 0.0)
        t = jnp.concatenate([t, jnp.zeros((8, LANES), jnp.float32)], axis=0)
        strip_z = strip_z + t
    edge_q = te * strip_q
    edge_z = te * strip_z

    for side in range(2):
        dx = c["dx"][side]
        acc = 0.0
        for k in range(vectors):
            at = (1 + side) * vectors + k
            start = (9 + k) * zdim
            acc = acc + dx[start : start + zdim, :] * yb[at : at + 1, :]
        c["bx"][side] = acc
    row8 = iota((8, LANES), 0)
    nothing = jnp.zeros((8, LANES), jnp.float32)
    for p in range(zdim + 1):
        b = p // zdim
        d_ref = c["d_own"] if b == 0 else c["d_other"]
        mxp, mxm, my = c["mxp"][b], c["mxm"][b], c["my"][b]
        q = scaled[p]
        tx, ty = c["tx"][p], c["ty"][p]
        acc = by_tiles(mxp, tx * x_next(q), (xdim // 8 - 1, xdim // 8))
        acc = acc + by_tiles(mxm, x_prev(tx * q), (0, xdim // 8))
        acc = acc + ty * y_next(q) + y_prev(ty * q)
        acc = acc + my * turn(edge_q, LANES - 6 - STRIDE * p, 1)
        acc = acc + c["tzlp"][p] * scaled[p + 1]
        if p > 0:
            acc = acc + c["tzlm"][p] * scaled[p - 1]
        z = (2.0 - RELAXATION) * q + c["s"][p] * acc
        field = 0.0
        at = 3 * b * vectors
        for k in range(vectors):
            field = field + d_ref[k, mirror(p % zdim, zdim)] * yb[at + k : at + k + 1, :]
        tile = nothing
        if b == 0:
            tile = jnp.where(row8 == 0, c["bx"][0, p : p + 1, :], 0.0)
            tile = jnp.where(row8 == 7, c["bx"][1, p : p + 1, :], tile)
            zown_ref[p] = (z[:xdim] + field)
        z_ref[p] = z + jnp.concatenate([field, tile], axis=0)

    lane = iota((rows, LANES), 1)
    edge = jnp.where((lane == 0) | (lane == LANES - 1), 1.0, 0.0)
    plane64, slot64 = plane_of[:xdim], slot_of[:xdim]
    rz = zw = zi = nothing
    sums = [nothing] * vectors
    packed = jnp.zeros((xdim, LANES), jnp.float32)
    for p in range(zdim):
        z = z_ref[p]
        tx, ty = c["tx"][p], c["ty"][p]
        acc = tx * x_next(z) + x_prev(tx * z)
        acc = acc + ty * y_next(z) + y_prev(ty * z)
        acc = acc + edge * turn(edge_z, LANES - 6 - STRIDE * p, 1)
        acc = acc + c["tz"][p] * z_ref[p + 1]
        if p > 0:
            acc = acc + c["tz"][p - 1] * z_ref[p - 1]
        w = (c["diag"][p] * z - acc)[:xdim]
        z = z[:xdim]
        w_ref[p] = w
        rz = rz + eights(r_ref[p][:xdim] * z)
        zw = zw + eights(w * z)
        if img_ref is not None:
            zi = zi + eights(img_ref[p][:xdim] * z)
        for k in range(vectors):
            sums[k] = sums[k] + eights(c["d_own"][k, mirror(p, zdim)] * w)
        moved = turn(w, STRIDE * p + 2, 1)
        packed = jnp.where((plane64 == p) & (slot64 < 4), moved, packed)

    acc_ref = c["acc"]
    acc_ref[...] = jnp.zeros(acc_ref.shape, jnp.float32)
    for j, value in list(enumerate(sums)) + [(16, rz), (17, zw), (18, zi)]:
        acc_ref[j : j + 1, :] = jnp.sum(value, axis=0, keepdims=True)
    row = spread_row(acc_ref)
    peers = send_ref.shape[0]
    if last:
        for p in range(peers):
            send_ref[p] = row
        return
    for p in range(peers):
        send_ref[p, zdim, 0:1, :] = row
    sw_ref[...] = packed
    zsend_ref[0] = w_ref[zdim - 1]
    zsend_ref[1] = w_ref[zdim - 2]
    for p in range(zdim):
        send_ref[ids[1], p] = w_ref[p, xdim - 2 : xdim, :]
        send_ref[ids[2], p] = w_ref[p, 0:2, :]
    part = xdim // 4
    pair = (iota((part, LANES), 1) & 7) >> 1
    to_hi = jnp.zeros((part, LANES), jnp.float32)
    to_lo = to_hi
    for g in range(4):
        rows_g = packed[g * part : (g + 1) * part]
        to_hi = jnp.where(pair == g, turn(rows_g, 2 * g, 1), to_hi)
        to_lo = jnp.where(pair == g, turn(rows_g, 2 * g - 2, 1), to_lo)
    for i in range(part // 2):
        send_ref[ids[3], i] = to_hi[2 * i : 2 * i + 2]
        send_ref[ids[4], i] = to_lo[2 * i : 2 * i + 2]
    for i in (5, 6):
        send_ref[ids[i], 0, 0:1, :] = packed[xdim - 1 : xdim, :]
    for i in (7, 8):
        send_ref[ids[i], 0, 0:1, :] = packed[0:1, :]


def first_kernel(zdim, xdim, *refs):
    (ids, near, s_own, s_hi, s_lo, d_own, d_other) = refs[0:7]
    dx = refs[7:11]
    (select, known_ref) = refs[11:13]
    fields = (refs[13:16], refs[16:19])
    refs = refs[19:]
    (send, w_ref, zown, sw, strips, tx, ty, tz, tzlp, tzlm, s_ref, diag_ref, mxp, mxm, my, rs_ref, r_full, zsend) = refs[:18]
    (scaled, z_ref, yb, acc, bx) = refs[18:23]
    rows = xdim + 8
    deep = zdim + 3
    shape = (rows, LANES)
    row, lane = iota(shape, 0), iota(shape, 1)
    plane_of, slot_of = place(shape)
    mirrored = ids[9] == 1

    def mg(col, b, d):
        at = 2 * col + b
        return near[at : at + 1, 16 + d : 17 + d]

    def facing(col, b, up):
        return jnp.where(mirrored, mg(col, b, 0 if up else 1), mg(col, b, 1 if up else 0))

    def z_by_row(b, up):
        beyond = jnp.where(row < xdim + 4, facing(1, b, up), facing(2, b, up))
        return jnp.where(row < xdim, facing(0, b, up), beyond)

    def by_row(b, d):
        return jnp.where(row < xdim, mg(0, b, d), jnp.where(row < xdim + 4, mg(1, b, d), mg(2, b, d)))

    for b in range(2):
        mxp[b] = jnp.where(row == xdim - 1, mg(0, b, 3), jnp.where(row == rows - 1, mg(2, b, 3), 1.0))
        mxm[b] = jnp.where(row == 0, mg(0, b, 2), jnp.where(row == xdim, mg(1, b, 2), 1.0))
        my[b] = jnp.where(lane == LANES - 1, by_row(b, 5), jnp.where(lane == 0, by_row(b, 4), 0.0))

    def strip(i):
        at = slice(i * rows, (i + 1) * rows)
        own, hi, lo = s_own[at, :], s_hi[at, :], s_lo[at, :]
        out = jnp.where((slot_of == 1) | (slot_of == 2), turn(own, -1, 1), 0.0)
        out = jnp.where(slot_of == 5, turn(hi, 2, 1), out)
        out = jnp.where(slot_of == 3, turn(hi, -1, 1), out)
        out = jnp.where(slot_of == 0, turn(hi, -5, 1), out)
        out = jnp.where(slot_of == 6, turn(lo, 4, 1), out)
        out = jnp.where(slot_of == 4, turn(lo, 3, 1), out)
        return jnp.where(slot_of == 7, turn(lo, 7, 1), out)

    ps, st, rs = strip(0), strip(1), strip(2)
    rs_ref[...] = rs
    face = (slot_of == 5) | (slot_of == 6)
    t_x = conduct(ps, x_next(ps))
    t_z = jnp.where(plane_of < deep - 1, conduct(ps, turn(ps, -STRIDE, 1)), 0.0)
    t_in = jnp.where(face, conduct(ps, turn(ps, 4, 1)), 0.0)
    t_out = jnp.where(face, conduct(ps, turn(ps, 2, 1)), 0.0)
    t_far = jnp.where(
        slot_of == 3,
        conduct(ps, turn(ps, 3, 1)),
        jnp.where(slot_of == 4, conduct(ps, turn(ps, -3, 1)), 0.0),
    )
    diag_s = st + t_x + x_prev(t_x) + t_z + turn(t_z, STRIDE, 1)
    diag_s = diag_s + t_in + t_out + turn(t_out, -2, 1) + t_far
    ss = jnp.where(diag_s > 0.0, RELAXATION / jnp.where(diag_s > 0.0, diag_s, 1.0), 0.0)

    def by_side(b, d_hi, d_lo):
        return jnp.where(slot_of == 5, mg(3, b, d_hi), mg(4, b, d_lo))

    def by_brick(d_hi, d_lo):
        return jnp.where(plane_of < zdim, by_side(0, d_hi, d_lo), by_side(1, d_hi, d_lo))

    def only(values):
        return jnp.where(face, values, 0.0)

    strips[0] = t_in
    strips[1] = only(t_x * jnp.where(row == xdim - 1, by_brick(3, 3), 1.0))
    strips[2] = only(x_prev(t_x) * jnp.where(row == 0, by_brick(2, 2), 1.0))
    strips[3] = t_in * by_brick(4, 5)
    strips[4] = t_out
    at_side = jnp.where(slot_of == 5, facing(3, 0, True), facing(4, 0, True))
    strips[5] = only(t_z * jnp.where(plane_of == zdim - 1, at_side, 1.0))
    strips[6] = only(jnp.where(plane_of == 0, 0.0, turn(t_z, STRIDE, 1)))

    inside = lane < LANES - 1

    for p in range(deep):
        scaled[p] = plane_of_field(fields, dx, 0, p)
        diag_ref[p] = plane_of_field(fields, dx, 1, p)
        r_full[p] = plane_of_field(fields, dx, 2, p)
    for p in range(deep - 1):
        here = scaled[p]
        tx[p] = conduct(here, x_next(here))
        ty[p] = jnp.where(inside, conduct(here, y_next(here)), 0.0)
        tz[p] = conduct(here, scaled[p + 1])
    edge = (lane == 0) | (lane == LANES - 1)
    inner = jnp.zeros(shape, jnp.float32)
    for p in range(deep - 1):
        t_x, t_y, t_z = tx[p], ty[p], tz[p]
        t_b = tz[p - 1] if p > 0 else jnp.zeros(shape, jnp.float32)
        total = diag_ref[p] + t_x + x_prev(t_x) + t_y + y_prev(t_y) + t_z + t_b
        total = total + jnp.where(edge, turn(t_in, LANES - 6 - STRIDE * p, 1), 0.0)
        relax = jnp.where(total > 0.0, RELAXATION / jnp.where(total > 0.0, total, 1.0), 0.0)
        diag_ref[p] = total
        s_ref[p] = relax
        tzlp[p] = t_z * z_by_row(0, True) if p == zdim - 1 else t_z
        tzlm[p] = t_b * z_by_row(1, False) if p == zdim else t_b
        scaled[p] = relax * r_full[p]
        if p < zdim:
            moved = turn(relax, STRIDE * p + 2, 1)
            inner = jnp.where((plane_of == p) & ((slot_of == 1) | (slot_of == 2)), moved, inner)
    ss = jnp.where((slot_of == 1) | (slot_of == 2), inner, ss)
    strips[7] = ss

    known = [known_ref[t : t + 1, :] for t in range(known_ref.shape[0])]
    solve_coarse(known, select, yb)
    c = dict(
        tx=tx, ty=ty, tz=tz, tzlp=tzlp, tzlm=tzlm, s=s_ref, diag=diag_ref, mxp=mxp, mxm=mxm, my=my,
        strips=strips, d_own=d_own, d_other=d_other, dx=dx, dy_hi=s_hi.at[3 * rows : 3 * rows + xdim, :],
        dy_lo=s_lo.at[3 * rows : 3 * rows + xdim, :], yb=yb, acc=acc, bx=bx,
    )
    finish(c, scaled, ss * rs, r_full, z_ref, send, w_ref, zown, sw, zsend, None, ids, False)


def totals(rows, count):
    lane = iota((1, LANES), 1)
    total = 0.0
    for i in range(count):
        total = total + (rows(i, 0) + rows(i, 1))
    sums = [
        jnp.sum(jnp.where(lane == 16 + j, total, 0.0), axis=1, keepdims=True) for j in range(3)
    ]
    tiles = []
    for t in range(count // 4):
        tile = jnp.zeros((1, LANES), jnp.float32)
        for i in range(4):
            for b in range(2):
                mine = (lane >> 3) == 4 * i + b
                tile = jnp.where(mine, turn(rows(4 * t + i, b), 8 * b, 1), tile)
        tiles.append(tile)
    return tiles, sums


def scalars(sums, scal_ref, first):
    inner = sums[0]
    if first:
        ratio = jnp.zeros_like(inner)
        curvature = sums[1]
    else:
        ratio = inner / scal_ref[0:1, 0:1]
        curvature = sums[1] + ratio * (2.0 * sums[2] + ratio * scal_ref[1:2, 0:1])
    return inner, ratio, curvature, inner / curvature


def next_kernel(zdim, xdim, first, last, *refs):
    refs = list(refs)

    def take(n):
        out, refs[:n] = refs[:n], []
        return out

    ids, got, far, zgot, d_own, d_other, *dx = take(10)
    s_hi, s_lo, select, strips, tx, ty, tz, tzlp, tzlm, s_ref, diag_ref, mxp, mxm, my = take(14)
    known_ref, w_in, z_in, sw_in, rs_in = take(5)
    if first:
        (r_in,) = take(1)
    else:
        r_in, img_in, dir_in, sol_in, is_in, kimg_ref, scal_ref = take(7)
    send, w_ref, zown, sw, rs_ref, r_ref, img_ref, dir_ref, sol_ref, is_ref, known_out, kimg_out, scal_out, zsend = take(14)
    scaled, z_ref, yb, acc, bx, tiles_ref = take(6)
    rows = xdim + 8
    plane_of, slot_of = place((rows, LANES))

    peers = got.shape[0]
    tiles, sums = totals(lambda i, b: (got, far)[b][i, zdim, 0:1, :], peers)
    inner, ratio, curvature, step = scalars(sums, None if first else scal_ref, first)
    scal_out[0:1, :] = jnp.broadcast_to(inner, (1, LANES))
    scal_out[1:2, :] = jnp.broadcast_to(curvature, (1, LANES))
    known = []
    for t, tile in enumerate(tiles):
        if not first:
            tile = tile + ratio * kimg_ref[t : t + 1, :]
        kimg_out[t : t + 1, :] = tile
        value = known_ref[t : t + 1, :] - step * tile
        known_out[t : t + 1, :] = value
        known.append(value)
    solve_coarse(known, select, yb)

    part = xdim // 4
    for i in range(part // 2):
        for j in range(4):
            tiles_ref[j, 2 * i : 2 * i + 2, :] = (got, far)[j // 2][ids[3 + j % 2], i]
    from_hi, from_lo, far_hi, far_lo = (tiles_ref[j] for j in range(4))
    beyond = plane_of[:part] == zdim
    own = sw_in[...]
    slot_part = slot_of[:part]
    blocks = []
    for g in range(4):
        value = own[g * part : (g + 1) * part]
        value = jnp.where(slot_part == 5, turn(from_hi, 5 - 2 * g, 1), value)
        value = jnp.where(slot_part == 3, turn(from_hi, 2 - 2 * g, 1), value)
        value = jnp.where(slot_part == 4, turn(from_lo, 4 - 2 * g, 1), value)
        value = jnp.where(slot_part == 6, turn(from_lo, 5 - 2 * g, 1), value)
        value = jnp.where(beyond & (slot_part == 5), turn(far_hi, STRIDE + 5 - 2 * g, 1), value)
        value = jnp.where(beyond & (slot_part == 6), turn(far_lo, STRIDE + 5 - 2 * g, 1), value)
        blocks.append(value)
    slot8, row8 = slot_of[:8], iota((8, LANES), 0)
    tile = jnp.zeros((8, LANES), jnp.float32)
    for i, at, want, shift in ((5, 0, 5, 3), (6, 0, 6, 5), (7, 7, 5, 3), (8, 7, 6, 5)):
        value = turn(jnp.broadcast_to(got[ids[i], 0, 0:1, :], (8, LANES)), shift, 1)
        tile = jnp.where((row8 == at) & (slot8 == want), value, tile)
    ws = jnp.concatenate(blocks + [tile], axis=0)
    ws = jnp.where((slot_of == 0) | (slot_of == 7), 0.0, ws)
    if not first:
        ws = ws + ratio * is_in[...]
    is_ref[...] = ws
    rs = rs_in[...] - step * ws
    rs_ref[...] = rs
    strip_q = strips[7] * rs

    tiles_ref[...] = jnp.zeros(tiles_ref.shape, jnp.float32)
    for p in range(zdim):
        tiles_ref[p, 0:2, :] = got[ids[1], p]
        tiles_ref[p, 6:8, :] = got[ids[2], p]
    tiles_ref[zdim, 0:1, :] = far[ids[1], zdim - 1, 0:1, :]
    tiles_ref[zdim, 7:8, :] = far[ids[2], zdim - 1, 1:2, :]
    for p in range(zdim + 2):
        inside = w_in[p] if p < zdim else zgot[p - zdim]
        image = jnp.concatenate([inside, tiles_ref[p, 0:8, :]], axis=0)
        if not first:
            image = image + ratio * img_in[p]
        img_ref[p] = image
        r = r_in[p] - step * image
        r_ref[p] = r
        scaled[p] = s_ref[p] * r
    for p in range(zdim):
        d = z_in[p]
        if first:
            sol_ref[p] = step * d
        else:
            d = d + ratio * dir_in[p]
            sol_ref[p] = sol_in[p] + step * d
        dir_ref[p] = d
    c = dict(
        tx=tx, ty=ty, tz=tz, tzlp=tzlp, tzlm=tzlm, s=s_ref, diag=diag_ref, mxp=mxp, mxm=mxm, my=my,
        strips=strips, d_own=d_own, d_other=d_other, dx=dx, dy_hi=s_hi.at[3 * rows : 3 * rows + xdim, :],
        dy_lo=s_lo.at[3 * rows : 3 * rows + xdim, :], yb=yb, acc=acc, bx=bx,
    )
    finish(c, scaled, strip_q, r_ref, z_ref, send, w_ref, zown, sw, zsend, img_ref, ids, last)


def last_kernel(zdim, xdim, got, w_in, z_in, r_in, img_in, dir_in, sol_in, scal_ref, sol_ref, r_ref):
    _, sums = totals(lambda i, b: got[2 * i + b], got.shape[0] // 2)
    _, ratio, _, step = scalars(sums, scal_ref, False)
    for p in range(zdim):
        at = mirror(p, zdim)
        image = w_in[p] + ratio * img_in[p][:xdim]
        r_ref[at] = r_in[p][:xdim] - step * image
        sol_ref[at] = sol_in[p] + step * (z_in[p] + ratio * dir_in[p])


def call(kernel, name, args, outs, scratch=(), smem=0):
    specs = [pl.BlockSpec(memory_space=pltpu.SMEM)] * smem
    specs += [pl.BlockSpec(memory_space=pltpu.VMEM)] * (len(args) - smem)
    return pl.pallas_call(
        kernel,
        name=name,
        in_specs=specs,
        out_specs=[pl.BlockSpec(memory_space=pltpu.VMEM)] * len(outs),
        out_shape=[jax.ShapeDtypeStruct(o, jnp.float32) for o in outs],
        scratch_shapes=[pltpu.VMEM(s, jnp.float32) for s in scratch],
        compiler_params=pltpu.CompilerParams(vmem_limit_bytes=24 * 1024 * 1024),
    )(*args)


def local(right_side, permeability, storage, deflation, coarse_inverse, owners, margin):
    nx, ny, nz = (lax.axis_size(a) for a in ("gx", "gy", "gz"))
    vectors, zdim, xdim, ydim = deflation.shape
    order = coarse_inverse.shape[1]
    assert nz == 2 and ydim == LANES and 2 * zdim * STRIDE == LANES and vectors == 8
    gx, gy, gz = (lax.axis_index(a) for a in ("gx", "gy", "gz"))
    peers, rows = nx * ny, xdim + 8
    me = gx * ny + gy
    off_x = jnp.array([0, 1, -1, 0, 0, 1, 1, -1, -1, 0], jnp.int32) + gx
    off_y = jnp.array([0, 0, 0, 1, -1, 1, -1, 1, -1, 0], jnp.int32) + gy
    there = (off_x >= 0) & (off_x < nx) & (off_y >= 0) & (off_y < ny)
    ids = jnp.where(there, off_x * ny + off_y, me)
    ids = jnp.where(jnp.arange(10) == 9, gz, ids)

    def swap(v):
        return lax.ppermute(v, "gz", [(0, 1), (1, 0)])

    def up(v, axis, count):
        return lax.ppermute(v, axis, [(i, i + 1) for i in range(count - 1)])

    def down(v, axis, count):
        return lax.ppermute(v, axis, [(i + 1, i) for i in range(count - 1)])

    fields = (permeability, storage, right_side)
    others = [swap(v) for v in fields]
    d_other = swap(deflation)
    edge_rows = ((9 + vectors) * zdim, LANES)
    first_row, x_up, x_down = call(
        lambda *refs: prep_kernel(zdim, xdim, *refs), "prep",
        [*fields, deflation, jnp.concatenate([owners.reshape(1, -1), margin.reshape(1, -1)], axis=1)],
        [(peers * nz, 1, LANES), edge_rows, edge_rows],
        [(PERIOD, LANES), (8, LANES)],
    )
    x_lo, x_hi = up(x_up, "gx", nx), down(x_down, "gx", nx)
    table = lax.all_to_all(first_row, ("gx", "gy", "gz"), 0, 0, tiled=True)
    dx = [x_hi, x_lo, swap(x_hi), swap(x_lo)]
    strip_rows = 3 * rows + xdim
    strip_hi, strip_lo = call(
        lambda *refs: pack_kernel(zdim, xdim, *refs), "pack",
        [*fields, *others, *dx, deflation],
        [(strip_rows, LANES), (strip_rows, LANES)],
    )
    s_lo = up(strip_hi, "gy", ny)
    s_hi = down(strip_lo, "gy", ny)
    coarse_inverse, _ = lax.optimization_barrier((coarse_inverse, strip_hi))
    whole = lax.all_gather(coarse_inverse, "gx", axis=0, tiled=True)
    tiles = peers * PERIOD // LANES
    select, known, near = call(
        coarse_kernel, "coarse", [ids, table, whole],
        [(10 * vectors, peers * PERIOD), (tiles, LANES), (16, LANES)],
        [(10 * vectors, order)], smem=1,
    )
    full, brick, one = (zdim + 3, rows, LANES), (zdim, xdim, LANES), (rows, LANES)
    mine, slots = (zdim, xdim, LANES), (peers, zdim + 1, 2, LANES)
    scratch = [full, full, (10 * vectors, LANES), (PERIOD, LANES), (2, zdim, LANES)]
    (send, w, z, sw, strips, *consts, rs, r_full, zsend) = call(
        lambda *refs: first_kernel(zdim, xdim, *refs), "first",
        [ids, near, strip_hi, s_hi, s_lo, deflation, d_other, *dx, select, known, *fields, *others],
        [slots, brick, mine, (xdim, LANES), (8, *one)] + [full] * 7 + [(2, *one)] * 3 + [one, full, (2, xdim, LANES)],
        scratch, smem=1,
    )
    state = [r_full]
    for iteration in range(ITERS - 1):
        first, last = iteration == 0, iteration == ITERS - 2
        got = lax.all_to_all(send, ("gx", "gy"), 0, 0, tiled=True)
        far, (zsend, _) = swap(got), lax.optimization_barrier((zsend, got))
        zgot = swap(zsend)
        send, w, z, sw, rs, r, img, direct, sol, ist, known, kimg, scal, zsend = call(
            lambda *refs: next_kernel(zdim, xdim, first, last, *refs), f"step{iteration}",
            [ids, got, far, zgot, deflation, d_other, *dx, s_hi, s_lo, select, strips, *consts, known, w, z, sw, rs, *state],
            [(peers * nz, 1, LANES) if last else slots, brick, mine, (xdim, LANES), one, full, full, mine, mine, one,
             (tiles, LANES), (tiles, LANES), (8, LANES), (2, xdim, LANES)],
            scratch + [(zdim + 2, max(8, xdim // 4), LANES)], smem=1,
        )
        state = [r, img, direct, sol, ist, kimg, scal]
    got = lax.all_to_all(send, ("gx", "gy", "gz"), 0, 0, tiled=True)
    return tuple(call(
        lambda *refs: last_kernel(zdim, xdim, *refs), "last",
        [got, w, z, r, img, direct, sol, scal], [mine, mine],
    ))


def solution(mesh):
    in_specs = (
        P("gz", "gx", "gy"),
        P("gz", "gx", "gy"),
        P("gz", "gx", "gy"),
        P(None, "gz", "gx", "gy"),
        P("gx", None),
        P("gz", "gx", "gy", None),
        P("gz", "gx", "gy", None),
    )
    out_specs = (P("gz", "gx", "gy"), P("gz", "gx", "gy"))
    return jax.shard_map(local, mesh=mesh, in_specs=in_specs, out_specs=out_specs, check_vma=False)
```

```python
import jax
import jax.numpy as jnp
from jax import lax
from jax.experimental import pallas as pl
from jax.experimental.pallas import tpu as pltpu
from jax.sharding import PartitionSpec as P

ITERS = 4
RELAXATION = 0.7
PRECISE = lax.Precision.HIGHEST
LANES = 128
STRIDE = 8
PERIOD = 32


def conduct(first_perm, second_perm):
    return 2.0 * first_perm * second_perm / jnp.maximum(first_perm + second_perm, 0.05)


def turn(values, shift, axis):
    size = values.shape[axis]
    if isinstance(shift, int):
        shift = shift % size
        if shift == 0:
            return values
    return pltpu.roll(values, shift, axis)


def rem(a, b):
    return a % b if isinstance(a, int) else lax.rem(a, b)


def x_next(v):
    return turn(v, -1, 0)


def x_prev(v):
    return turn(v, 1, 0)


def y_next(v):
    return turn(v, -1, 1)


def y_prev(v):
    return turn(v, 1, 1)


def iota(shape, dim):
    return lax.broadcasted_iota(jnp.int32, shape, dim)


def place(shape):
    lane = iota(shape, 1)
    return lane >> 3, lane & 7


def mirror(p, zdim):
    return p + lax.axis_index("gz") * (zdim - 1 - 2 * p)


def by_tiles(mask, values, tiles):
    parts, at = [], 0
    for t in tiles:
        if 8 * t > at:
            parts.append(values[at : 8 * t])
        at = 8 * (t + 1)
        parts.append(mask[8 * t : at] * values[8 * t : at])
    if at < values.shape[0]:
        parts.append(values[at:])
    return jnp.concatenate(parts, axis=0)


def eights(values):
    out = values[0:8]
    for t in range(1, values.shape[0] // 8):
        out = out + values[8 * t : 8 * t + 8]
    return out


def spread_row(acc_ref):
    count = acc_ref.shape[0]
    column = jnp.broadcast_to(jnp.sum(acc_ref[...], axis=1, keepdims=True), (count, LANES))
    match = iota((count, LANES), 0) == (iota((count, LANES), 1) & (count - 1))
    return jnp.sum(jnp.where(match, column, 0.0), axis=0, keepdims=True)


def prep_kernel(zdim, xdim, perm, stor, resid, d, owners, margin, whole, row_ref, up_ref, down_ref, acc, line):
    for f, field in enumerate((perm, stor, resid)):
        for pz in range(zdim):
            at = (f * zdim + pz) * 3
            up_ref[at : at + 3, :] = field[mirror(pz, zdim), xdim - 3 : xdim, :]
            down_ref[at : at + 3, :] = field[mirror(pz, zdim), 0:3, :]
    vectors = d.shape[0]
    acc[...] = jnp.zeros(acc.shape, jnp.float32)
    for k in range(vectors):
        total = jnp.zeros((8, LANES), jnp.float32)
        for pz in range(zdim):
            at = (9 + k) * zdim + pz
            up_ref[at : at + 1, :] = d[k, mirror(pz, zdim), xdim - 1 : xdim, :]
            down_ref[at : at + 1, :] = d[k, mirror(pz, zdim), 0:1, :]
            total = total + eights(d[k, pz] * resid[pz])
        acc[k : k + 1, :] = jnp.sum(total, axis=0, keepdims=True)
    line[...] = jnp.zeros(line.shape, jnp.float32)
    line[0:1, 8 : 8 + vectors] = owners[...].astype(jnp.float32)
    line[0:1, 16:22] = margin[...].astype(jnp.float32)
    extra = line[0:1, :]
    extra = extra + turn(extra, PERIOD, 1)
    extra = extra + turn(extra, 2 * PERIOD, 1)
    row = spread_row(acc) + extra
    share, halves = row_ref.shape[1] - 1, row_ref.shape[2]
    block = lax.axis_index("gy") * lax.axis_size("gz") + lax.axis_index("gz")
    piece = whole[pl.ds(pl.multiple_of(block * share, 8), share), :]
    for p in range(row_ref.shape[0]):
        row_ref[p, share, 0:1, :] = row
        for h in range(halves):
            row_ref[p, 0:share, h, :] = piece[:, LANES * h : LANES * (h + 1)]


def coarse_kernel(ids, table, select, known_ref, near, hot, whole):
    order = whole.shape[0]
    share = table.shape[1] - 1
    for p in range(table.shape[0]):
        for h in range(table.shape[2]):
            whole[share * p : share * (p + 1), LANES * h : LANES * (h + 1)] = table[p, 0:share, h, :]
    zb = ids[9]
    place_of = (zb, 1 - zb)
    lane = iota((1, LANES), 1)
    lane8, sub8 = iota((8, LANES), 1), iota((8, LANES), 0)
    number = iota((8, order), 1).astype(jnp.float32)
    near[...] = jnp.zeros(near.shape, jnp.float32)
    for col in range(5):
        for b in range(2):
            row = table[2 * ids[col] + place_of[b], share, 0:1, :]
            near[2 * col + b : 2 * col + b + 1, :] = row
            owner = jnp.sum(jnp.where(lane8 == sub8 + 8, row, 0.0), axis=1, keepdims=True)
            at = 8 * (3 * b + col if col < 3 else 2 * col + b)
            hot[at : at + 8, :] = (number == owner).astype(jnp.float32)
    rows = jnp.dot(hot[...], whole[...], precision=PRECISE, preferred_element_type=jnp.float32)
    index = iota((order, LANES), 0).astype(jnp.float32)
    for t in range(known_ref.shape[0]):
        known = jnp.zeros((1, LANES), jnp.float32)
        owner = known - 1.0
        for i in range(4):
            for b in range(2):
                row = table[2 * (4 * t + i) + place_of[b], share, 0:1, :]
                mine = (lane >> 3) == 4 * i + b
                known = jnp.where(mine, turn(row, 8 * b, 1), known)
                owner = jnp.where(mine, turn(row, 8 * b - 8, 1), owner)
        known_ref[t : t + 1, :] = known
        pick = (index == owner).astype(jnp.float32)
        select[:, LANES * t : LANES * (t + 1)] = jnp.dot(
            rows, pick, precision=PRECISE, preferred_element_type=jnp.float32
        )


def plane_of_field(fields, halos, f, p):
    own, other = fields
    zdim, xdim = own[0].shape[0], own[0].shape[1]
    hi_own, lo_own, hi_other, lo_other = halos
    src, hi, lo = (own, hi_own, lo_own) if p < zdim else (other, hi_other, lo_other)
    at = (f * zdim + (p if p < zdim else 2 * zdim - 1 - p)) * 3
    gap = jnp.zeros((2, LANES), jnp.float32)
    tile = jnp.concatenate([hi[at : at + 3, :], gap, lo[at : at + 3, :]], axis=0)
    return jnp.concatenate([src[f][mirror(p % zdim, zdim)], tile], axis=0)


def pack_kernel(zdim, xdim, *refs):
    fields = (refs[0:3], refs[3:6])
    halos, d_own = refs[6:10], refs[10]
    strip_hi, strip_lo = refs[11:13]
    rows = xdim + 8
    shape = (rows, LANES)
    plane_of, slot_of = place(shape)
    for f in range(3):
        acc = jnp.zeros(shape, jnp.float32)
        for p in range(zdim + 3):
            moved = turn(plane_of_field(fields, halos, f, p), STRIDE * p + 3, 1)
            acc = jnp.where((plane_of == p) & (slot_of < 6), moved, acc)
        strip_hi[f * rows : (f + 1) * rows, :] = acc
        strip_lo[f * rows : (f + 1) * rows, :] = acc
    lane = iota((xdim, LANES), 1)
    vectors = d_own.shape[0]
    hi_acc = jnp.zeros((xdim, LANES), jnp.float32)
    lo_acc = hi_acc
    for k in range(vectors):
        for p in range(zdim):
            at = STRIDE * p + k
            moved = turn(d_own[k, mirror(p, zdim)], at + 1, 1)
            hi_acc = jnp.where(lane == at, moved, hi_acc)
            lo_acc = jnp.where(lane == at + 1, moved, lo_acc)
    strip_hi[3 * rows : 3 * rows + xdim, :] = hi_acc
    strip_lo[3 * rows : 3 * rows + xdim, :] = turn(lo_acc, -1, 1)


def solve_coarse(known, select_ref, yb_ref):
    total = 0.0
    for t, row in enumerate(known):
        total = total + select_ref[:, LANES * t : LANES * (t + 1)] * row
    column = jnp.sum(total, axis=1, keepdims=True)
    yb_ref[...] = jnp.broadcast_to(column, yb_ref.shape)


def finish(c, scaled, strip_q, r_ref, z_ref, send_ref, w_ref, zown_ref, sw_ref, zsend_ref, img_ref, ids, last):
    zdim, xdim = c["d_own"].shape[1], c["d_own"].shape[2]
    rows = xdim + 8
    vectors = c["d_own"].shape[0]
    strips = c["strips"]
    yb = c["yb"]
    plane_of, slot_of = place((rows, LANES))

    te, cxp, cxm, cin, cout, czp, czm, ss = (strips[i] for i in range(8))
    smooth = (
        cxp * x_next(strip_q)
        + cxm * x_prev(strip_q)
        + cin * turn(strip_q, 4, 1)
        + cout * turn(strip_q, 2, 1)
        + czp * turn(strip_q, -STRIDE, 1)
        + czm * turn(strip_q, STRIDE, 1)
    )
    strip_z = (2.0 - RELAXATION) * strip_q + ss * smooth
    lane8, row8 = iota((vectors, LANES), 1), iota((vectors, LANES), 0)
    wanted = row8 == (lane8 & 7)
    for side, d_strip in ((0, c["dy_hi"]), (1, c["dy_lo"])):
        at = 6 * vectors + side * 2 * vectors
        coeff = jnp.sum(jnp.where(wanted, yb[at : at + vectors, :], 0.0), axis=0, keepdims=True)
        t = d_strip[...] * coeff
        t = t + turn(t, -1, 1)
        t = t + turn(t, -2, 1)
        t = t + turn(t, -4, 1)
        t = jnp.where(slot_of[:xdim] == 5 + side, turn(t, 5 + side, 1), 0.0)
        t = jnp.concatenate([t, jnp.zeros((8, LANES), jnp.float32)], axis=0)
        strip_z = strip_z + t
    edge_q = te * strip_q
    edge_z = te * strip_z

    for side in range(2):
        dx = c["dx"][side]
        acc = 0.0
        for k in range(vectors):
            at = (1 + side) * vectors + k
            start = (9 + k) * zdim
            acc = acc + dx[start : start + zdim, :] * yb[at : at + 1, :]
        c["bx"][side] = acc
    row8 = iota((8, LANES), 0)
    nothing = jnp.zeros((8, LANES), jnp.float32)
    for p in range(zdim + 1):
        b = p // zdim
        d_ref = c["d_own"] if b == 0 else c["d_other"]
        mxp, mxm, my = c["mxp"][b], c["mxm"][b], c["my"][b]
        q = scaled[p]
        tx, ty = c["tx"][p], c["ty"][p]
        acc = by_tiles(mxp, tx * x_next(q), (xdim // 8 - 1, xdim // 8))
        acc = acc + by_tiles(mxm, x_prev(tx * q), (0, xdim // 8))
        acc = acc + ty * y_next(q) + y_prev(ty * q)
        acc = acc + my * turn(edge_q, LANES - 6 - STRIDE * p, 1)
        acc = acc + c["tzlp"][p] * scaled[p + 1]
        if p > 0:
            acc = acc + c["tzlm"][p] * scaled[p - 1]
        z = (2.0 - RELAXATION) * q + c["s"][p] * acc
        field = 0.0
        at = 3 * b * vectors
        for k in range(vectors):
            field = field + d_ref[k, mirror(p % zdim, zdim)] * yb[at + k : at + k + 1, :]
        tile = nothing
        if b == 0:
            tile = jnp.where(row8 == 0, c["bx"][0, p : p + 1, :], 0.0)
            tile = jnp.where(row8 == 7, c["bx"][1, p : p + 1, :], tile)
            zown_ref[p] = (z[:xdim] + field)
        z_ref[p] = z + jnp.concatenate([field, tile], axis=0)

    lane = iota((rows, LANES), 1)
    edge = jnp.where((lane == 0) | (lane == LANES - 1), 1.0, 0.0)
    plane64, slot64 = plane_of[:xdim], slot_of[:xdim]
    rz = zw = zi = nothing
    sums = [nothing] * vectors
    packed = jnp.zeros((xdim, LANES), jnp.float32)
    for p in range(zdim):
        z = z_ref[p]
        tx, ty = c["tx"][p], c["ty"][p]
        acc = tx * x_next(z) + x_prev(tx * z)
        acc = acc + ty * y_next(z) + y_prev(ty * z)
        acc = acc + edge * turn(edge_z, LANES - 6 - STRIDE * p, 1)
        acc = acc + c["tz"][p] * z_ref[p + 1]
        if p > 0:
            acc = acc + c["tz"][p - 1] * z_ref[p - 1]
        w = (c["diag"][p] * z - acc)[:xdim]
        z = z[:xdim]
        w_ref[p] = w
        rz = rz + eights(r_ref[p][:xdim] * z)
        zw = zw + eights(w * z)
        if img_ref is not None:
            zi = zi + eights(img_ref[p][:xdim] * z)
        for k in range(vectors):
            sums[k] = sums[k] + eights(c["d_own"][k, mirror(p, zdim)] * w)
        moved = turn(w, STRIDE * p + 2, 1)
        packed = jnp.where((plane64 == p) & (slot64 < 4), moved, packed)

    acc_ref = c["acc"]
    acc_ref[...] = jnp.zeros(acc_ref.shape, jnp.float32)
    for j, value in list(enumerate(sums)) + [(16, rz), (17, zw), (18, zi)]:
        acc_ref[j : j + 1, :] = jnp.sum(value, axis=0, keepdims=True)
    row = spread_row(acc_ref)
    peers = send_ref.shape[0]
    if last:
        for p in range(peers):
            send_ref[p] = row
        return
    for p in range(peers):
        send_ref[p, zdim, 0:1, :] = row
    sw_ref[...] = packed
    zsend_ref[0] = w_ref[zdim - 1]
    zsend_ref[1] = w_ref[zdim - 2]
    for p in range(zdim):
        send_ref[ids[1], p] = w_ref[p, xdim - 2 : xdim, :]
        send_ref[ids[2], p] = w_ref[p, 0:2, :]
    part = xdim // 4
    pair = (iota((part, LANES), 1) & 7) >> 1
    to_hi = jnp.zeros((part, LANES), jnp.float32)
    to_lo = to_hi
    for g in range(4):
        rows_g = packed[g * part : (g + 1) * part]
        to_hi = jnp.where(pair == g, turn(rows_g, 2 * g, 1), to_hi)
        to_lo = jnp.where(pair == g, turn(rows_g, 2 * g - 2, 1), to_lo)
    for i in range(part // 2):
        send_ref[ids[3], i] = to_hi[2 * i : 2 * i + 2]
        send_ref[ids[4], i] = to_lo[2 * i : 2 * i + 2]
    for i in (5, 6):
        send_ref[ids[i], 0, 0:1, :] = packed[xdim - 1 : xdim, :]
    for i in (7, 8):
        send_ref[ids[i], 0, 0:1, :] = packed[0:1, :]


def first_kernel(zdim, xdim, *refs):
    (ids, near, s_own, s_hi, s_lo, d_own, d_other) = refs[0:7]
    dx = refs[7:11]
    (select, known_ref) = refs[11:13]
    fields = (refs[13:16], refs[16:19])
    refs = refs[19:]
    (send, w_ref, zown, sw, strips, tx, ty, tz, tzlp, tzlm, s_ref, diag_ref, mxp, mxm, my, rs_ref, r_full, zsend) = refs[:18]
    (scaled, z_ref, yb, acc, bx) = refs[18:23]
    rows = xdim + 8
    deep = zdim + 3
    shape = (rows, LANES)
    row, lane = iota(shape, 0), iota(shape, 1)
    plane_of, slot_of = place(shape)
    mirrored = ids[9] == 1

    def mg(col, b, d):
        at = 2 * col + b
        return near[at : at + 1, 16 + d : 17 + d]

    def facing(col, b, up):
        return jnp.where(mirrored, mg(col, b, 0 if up else 1), mg(col, b, 1 if up else 0))

    def z_by_row(b, up):
        beyond = jnp.where(row < xdim + 4, facing(1, b, up), facing(2, b, up))
        return jnp.where(row < xdim, facing(0, b, up), beyond)

    def by_row(b, d):
        return jnp.where(row < xdim, mg(0, b, d), jnp.where(row < xdim + 4, mg(1, b, d), mg(2, b, d)))

    for b in range(2):
        mxp[b] = jnp.where(row == xdim - 1, mg(0, b, 3), jnp.where(row == rows - 1, mg(2, b, 3), 1.0))
        mxm[b] = jnp.where(row == 0, mg(0, b, 2), jnp.where(row == xdim, mg(1, b, 2), 1.0))
        my[b] = jnp.where(lane == LANES - 1, by_row(b, 5), jnp.where(lane == 0, by_row(b, 4), 0.0))

    def strip(i):
        at = slice(i * rows, (i + 1) * rows)
        own, hi, lo = s_own[at, :], s_hi[at, :], s_lo[at, :]
        out = jnp.where((slot_of == 1) | (slot_of == 2), turn(own, -1, 1), 0.0)
        out = jnp.where(slot_of == 5, turn(hi, 2, 1), out)
        out = jnp.where(slot_of == 3, turn(hi, -1, 1), out)
        out = jnp.where(slot_of == 0, turn(hi, -5, 1), out)
        out = jnp.where(slot_of == 6, turn(lo, 4, 1), out)
        out = jnp.where(slot_of == 4, turn(lo, 3, 1), out)
        return jnp.where(slot_of == 7, turn(lo, 7, 1), out)

    ps, st, rs = strip(0), strip(1), strip(2)
    rs_ref[...] = rs
    face = (slot_of == 5) | (slot_of == 6)
    t_x = conduct(ps, x_next(ps))
    t_z = jnp.where(plane_of < deep - 1, conduct(ps, turn(ps, -STRIDE, 1)), 0.0)
    t_in = jnp.where(face, conduct(ps, turn(ps, 4, 1)), 0.0)
    t_out = jnp.where(face, conduct(ps, turn(ps, 2, 1)), 0.0)
    t_far = jnp.where(
        slot_of == 3,
        conduct(ps, turn(ps, 3, 1)),
        jnp.where(slot_of == 4, conduct(ps, turn(ps, -3, 1)), 0.0),
    )
    diag_s = st + t_x + x_prev(t_x) + t_z + turn(t_z, STRIDE, 1)
    diag_s = diag_s + t_in + t_out + turn(t_out, -2, 1) + t_far
    ss = jnp.where(diag_s > 0.0, RELAXATION / jnp.where(diag_s > 0.0, diag_s, 1.0), 0.0)

    def by_side(b, d_hi, d_lo):
        return jnp.where(slot_of == 5, mg(3, b, d_hi), mg(4, b, d_lo))

    def by_brick(d_hi, d_lo):
        return jnp.where(plane_of < zdim, by_side(0, d_hi, d_lo), by_side(1, d_hi, d_lo))

    def only(values):
        return jnp.where(face, values, 0.0)

    strips[0] = t_in
    strips[1] = only(t_x * jnp.where(row == xdim - 1, by_brick(3, 3), 1.0))
    strips[2] = only(x_prev(t_x) * jnp.where(row == 0, by_brick(2, 2), 1.0))
    strips[3] = t_in * by_brick(4, 5)
    strips[4] = t_out
    at_side = jnp.where(slot_of == 5, facing(3, 0, True), facing(4, 0, True))
    strips[5] = only(t_z * jnp.where(plane_of == zdim - 1, at_side, 1.0))
    strips[6] = only(jnp.where(plane_of == 0, 0.0, turn(t_z, STRIDE, 1)))

    inside = lane < LANES - 1

    for p in range(deep):
        scaled[p] = plane_of_field(fields, dx, 0, p)
        diag_ref[p] = plane_of_field(fields, dx, 1, p)
        r_full[p] = plane_of_field(fields, dx, 2, p)
    for p in range(deep - 1):
        here = scaled[p]
        tx[p] = conduct(here, x_next(here))
        ty[p] = jnp.where(inside, conduct(here, y_next(here)), 0.0)
        tz[p] = conduct(here, scaled[p + 1])
    edge = (lane == 0) | (lane == LANES - 1)
    inner = jnp.zeros(shape, jnp.float32)
    for p in range(deep - 1):
        t_x, t_y, t_z = tx[p], ty[p], tz[p]
        t_b = tz[p - 1] if p > 0 else jnp.zeros(shape, jnp.float32)
        total = diag_ref[p] + t_x + x_prev(t_x) + t_y + y_prev(t_y) + t_z + t_b
        total = total + jnp.where(edge, turn(t_in, LANES - 6 - STRIDE * p, 1), 0.0)
        relax = jnp.where(total > 0.0, RELAXATION / jnp.where(total > 0.0, total, 1.0), 0.0)
        diag_ref[p] = total
        s_ref[p] = relax
        tzlp[p] = t_z * z_by_row(0, True) if p == zdim - 1 else t_z
        tzlm[p] = t_b * z_by_row(1, False) if p == zdim else t_b
        scaled[p] = relax * r_full[p]
        if p < zdim:
            moved = turn(relax, STRIDE * p + 2, 1)
            inner = jnp.where((plane_of == p) & ((slot_of == 1) | (slot_of == 2)), moved, inner)
    ss = jnp.where((slot_of == 1) | (slot_of == 2), inner, ss)
    strips[7] = ss

    known = [known_ref[t : t + 1, :] for t in range(known_ref.shape[0])]
    solve_coarse(known, select, yb)
    c = dict(
        tx=tx, ty=ty, tz=tz, tzlp=tzlp, tzlm=tzlm, s=s_ref, diag=diag_ref, mxp=mxp, mxm=mxm, my=my,
        strips=strips, d_own=d_own, d_other=d_other, dx=dx, dy_hi=s_hi.at[3 * rows : 3 * rows + xdim, :],
        dy_lo=s_lo.at[3 * rows : 3 * rows + xdim, :], yb=yb, acc=acc, bx=bx,
    )
    finish(c, scaled, ss * rs, r_full, z_ref, send, w_ref, zown, sw, zsend, None, ids, False)


def totals(rows, count):
    lane = iota((1, LANES), 1)
    total = 0.0
    for i in range(count):
        total = total + (rows(i, 0) + rows(i, 1))
    sums = [
        jnp.sum(jnp.where(lane == 16 + j, total, 0.0), axis=1, keepdims=True) for j in range(3)
    ]
    tiles = []
    for t in range(count // 4):
        tile = jnp.zeros((1, LANES), jnp.float32)
        for i in range(4):
            for b in range(2):
                mine = (lane >> 3) == 4 * i + b
                tile = jnp.where(mine, turn(rows(4 * t + i, b), 8 * b, 1), tile)
        tiles.append(tile)
    return tiles, sums


def scalars(sums, scal_ref, first):
    inner = sums[0]
    if first:
        ratio = jnp.zeros_like(inner)
        curvature = sums[1]
    else:
        ratio = inner / scal_ref[0:1, 0:1]
        curvature = sums[1] + ratio * (2.0 * sums[2] + ratio * scal_ref[1:2, 0:1])
    return inner, ratio, curvature, inner / curvature


def next_kernel(zdim, xdim, first, last, *refs):
    refs = list(refs)

    def take(n):
        out, refs[:n] = refs[:n], []
        return out

    ids, got, far, zgot, d_own, d_other, *dx = take(10)
    s_hi, s_lo, select, strips, tx, ty, tz, tzlp, tzlm, s_ref, diag_ref, mxp, mxm, my = take(14)
    known_ref, w_in, z_in, sw_in, rs_in = take(5)
    if first:
        (r_in,) = take(1)
    else:
        r_in, img_in, dir_in, sol_in, is_in, kimg_ref, scal_ref = take(7)
    send, w_ref, zown, sw, rs_ref, r_ref, img_ref, dir_ref, sol_ref, is_ref, known_out, kimg_out, scal_out, zsend = take(14)
    scaled, z_ref, yb, acc, bx, tiles_ref = take(6)
    rows = xdim + 8
    plane_of, slot_of = place((rows, LANES))

    peers = got.shape[0]
    tiles, sums = totals(lambda i, b: (got, far)[b][i, zdim, 0:1, :], peers)
    inner, ratio, curvature, step = scalars(sums, None if first else scal_ref, first)
    scal_out[0:1, :] = jnp.broadcast_to(inner, (1, LANES))
    scal_out[1:2, :] = jnp.broadcast_to(curvature, (1, LANES))
    known = []
    for t, tile in enumerate(tiles):
        if not first:
            tile = tile + ratio * kimg_ref[t : t + 1, :]
        kimg_out[t : t + 1, :] = tile
        value = known_ref[t : t + 1, :] - step * tile
        known_out[t : t + 1, :] = value
        known.append(value)
    solve_coarse(known, select, yb)

    part = xdim // 4
    for i in range(part // 2):
        for j in range(4):
            tiles_ref[j, 2 * i : 2 * i + 2, :] = (got, far)[j // 2][ids[3 + j % 2], i]
    from_hi, from_lo, far_hi, far_lo = (tiles_ref[j] for j in range(4))
    beyond = plane_of[:part] == zdim
    own = sw_in[...]
    slot_part = slot_of[:part]
    blocks = []
    for g in range(4):
        value = own[g * part : (g + 1) * part]
        value = jnp.where(slot_part == 5, turn(from_hi, 5 - 2 * g, 1), value)
        value = jnp.where(slot_part == 3, turn(from_hi, 2 - 2 * g, 1), value)
        value = jnp.where(slot_part == 4, turn(from_lo, 4 - 2 * g, 1), value)
        value = jnp.where(slot_part == 6, turn(from_lo, 5 - 2 * g, 1), value)
        value = jnp.where(beyond & (slot_part == 5), turn(far_hi, STRIDE + 5 - 2 * g, 1), value)
        value = jnp.where(beyond & (slot_part == 6), turn(far_lo, STRIDE + 5 - 2 * g, 1), value)
        blocks.append(value)
    slot8, row8 = slot_of[:8], iota((8, LANES), 0)
    tile = jnp.zeros((8, LANES), jnp.float32)
    for i, at, want, shift in ((5, 0, 5, 3), (6, 0, 6, 5), (7, 7, 5, 3), (8, 7, 6, 5)):
        value = turn(jnp.broadcast_to(got[ids[i], 0, 0:1, :], (8, LANES)), shift, 1)
        tile = jnp.where((row8 == at) & (slot8 == want), value, tile)
    ws = jnp.concatenate(blocks + [tile], axis=0)
    ws = jnp.where((slot_of == 0) | (slot_of == 7), 0.0, ws)
    if not first:
        ws = ws + ratio * is_in[...]
    is_ref[...] = ws
    rs = rs_in[...] - step * ws
    rs_ref[...] = rs
    strip_q = strips[7] * rs

    tiles_ref[...] = jnp.zeros(tiles_ref.shape, jnp.float32)
    for p in range(zdim):
        tiles_ref[p, 0:2, :] = got[ids[1], p]
        tiles_ref[p, 6:8, :] = got[ids[2], p]
    tiles_ref[zdim, 0:1, :] = far[ids[1], zdim - 1, 0:1, :]
    tiles_ref[zdim, 7:8, :] = far[ids[2], zdim - 1, 1:2, :]
    for p in range(zdim + 2):
        inside = w_in[p] if p < zdim else zgot[p - zdim]
        image = jnp.concatenate([inside, tiles_ref[p, 0:8, :]], axis=0)
        if not first:
            image = image + ratio * img_in[p]
        img_ref[p] = image
        r = r_in[p] - step * image
        r_ref[p] = r
        scaled[p] = s_ref[p] * r
    for p in range(zdim):
        d = z_in[p]
        if first:
            sol_ref[p] = step * d
        else:
            d = d + ratio * dir_in[p]
            sol_ref[p] = sol_in[p] + step * d
        dir_ref[p] = d
    c = dict(
        tx=tx, ty=ty, tz=tz, tzlp=tzlp, tzlm=tzlm, s=s_ref, diag=diag_ref, mxp=mxp, mxm=mxm, my=my,
        strips=strips, d_own=d_own, d_other=d_other, dx=dx, dy_hi=s_hi.at[3 * rows : 3 * rows + xdim, :],
        dy_lo=s_lo.at[3 * rows : 3 * rows + xdim, :], yb=yb, acc=acc, bx=bx,
    )
    finish(c, scaled, strip_q, r_ref, z_ref, send, w_ref, zown, sw, zsend, img_ref, ids, last)


def last_kernel(zdim, xdim, got, w_in, z_in, r_in, img_in, dir_in, sol_in, scal_ref, sol_ref, r_ref):
    _, sums = totals(lambda i, b: got[2 * i + b], got.shape[0] // 2)
    _, ratio, _, step = scalars(sums, scal_ref, False)
    for p in range(zdim):
        at = mirror(p, zdim)
        image = w_in[p] + ratio * img_in[p][:xdim]
        r_ref[at] = r_in[p][:xdim] - step * image
        sol_ref[at] = sol_in[p] + step * (z_in[p] + ratio * dir_in[p])


def call(kernel, name, args, outs, scratch=(), smem=0, limit=24):
    specs = [pl.BlockSpec(memory_space=pltpu.SMEM)] * smem
    specs += [pl.BlockSpec(memory_space=pltpu.VMEM)] * (len(args) - smem)
    return pl.pallas_call(
        kernel,
        name=name,
        in_specs=specs,
        out_specs=[pl.BlockSpec(memory_space=pltpu.VMEM)] * len(outs),
        out_shape=[jax.ShapeDtypeStruct(o, jnp.float32) for o in outs],
        scratch_shapes=[pltpu.VMEM(s, jnp.float32) for s in scratch],
        compiler_params=pltpu.CompilerParams(vmem_limit_bytes=limit * 1024 * 1024),
    )(*args)


def local(right_side, permeability, storage, deflation, coarse_inverse, owners, margin):
    nx, ny, nz = (lax.axis_size(a) for a in ("gx", "gy", "gz"))
    vectors, zdim, xdim, ydim = deflation.shape
    order = coarse_inverse.shape[1]
    assert nz == 2 and ydim == LANES and 2 * zdim * STRIDE == LANES and vectors == 8
    gx, gy, gz = (lax.axis_index(a) for a in ("gx", "gy", "gz"))
    peers, rows = nx * ny, xdim + 8
    me = gx * ny + gy
    off_x = jnp.array([0, 1, -1, 0, 0, 1, 1, -1, -1, 0], jnp.int32) + gx
    off_y = jnp.array([0, 0, 0, 1, -1, 1, -1, 1, -1, 0], jnp.int32) + gy
    there = (off_x >= 0) & (off_x < nx) & (off_y >= 0) & (off_y < ny)
    ids = jnp.where(there, off_x * ny + off_y, me)
    ids = jnp.where(jnp.arange(10) == 9, gz, ids)

    def swap(v):
        return lax.ppermute(v, "gz", [(0, 1), (1, 0)])

    def up(v, axis, count):
        return lax.ppermute(v, axis, [(i, i + 1) for i in range(count - 1)])

    def down(v, axis, count):
        return lax.ppermute(v, axis, [(i + 1, i) for i in range(count - 1)])

    fields = (permeability, storage, right_side)
    others = [swap(v) for v in fields]
    d_other = swap(deflation)
    edge_rows = ((9 + vectors) * zdim, LANES)
    share = coarse_inverse.shape[0] // (ny * nz)
    assert share % 8 == 0
    first_row, x_up, x_down = call(
        lambda *refs: prep_kernel(zdim, xdim, *refs), "prep",
        [*fields, deflation, owners.reshape(1, -1), margin.reshape(1, -1), coarse_inverse],
        [(peers * nz, share + 1, order // LANES, LANES), edge_rows, edge_rows],
        [(PERIOD, LANES), (8, LANES)],
        limit=60,
    )
    x_lo, x_hi = up(x_up, "gx", nx), down(x_down, "gx", nx)
    table = lax.all_to_all(first_row, ("gx", "gy", "gz"), 0, 0, tiled=True)
    dx = [x_hi, x_lo, swap(x_hi), swap(x_lo)]
    strip_rows = 3 * rows + xdim
    strip_hi, strip_lo = call(
        lambda *refs: pack_kernel(zdim, xdim, *refs), "pack",
        [*fields, *others, *dx, deflation],
        [(strip_rows, LANES), (strip_rows, LANES)],
    )
    s_lo = up(strip_hi, "gy", ny)
    s_hi = down(strip_lo, "gy", ny)
    tiles = peers * PERIOD // LANES
    select, known, near = call(
        coarse_kernel, "coarse", [ids, table],
        [(10 * vectors, peers * PERIOD), (tiles, LANES), (16, LANES)],
        [(10 * vectors, order), (order, order)], smem=1,
    )
    full, brick, one = (zdim + 3, rows, LANES), (zdim, xdim, LANES), (rows, LANES)
    mine, slots = (zdim, xdim, LANES), (peers, zdim + 1, 2, LANES)
    scratch = [full, full, (10 * vectors, LANES), (PERIOD, LANES), (2, zdim, LANES)]
    (send, w, z, sw, strips, *consts, rs, r_full, zsend) = call(
        lambda *refs: first_kernel(zdim, xdim, *refs), "first",
        [ids, near, strip_hi, s_hi, s_lo, deflation, d_other, *dx, select, known, *fields, *others],
        [slots, brick, mine, (xdim, LANES), (8, *one)] + [full] * 7 + [(2, *one)] * 3 + [one, full, (2, xdim, LANES)],
        scratch, smem=1,
    )
    state = [r_full]
    for iteration in range(ITERS - 1):
        first, last = iteration == 0, iteration == ITERS - 2
        got = lax.all_to_all(send, ("gx", "gy"), 0, 0, tiled=True)
        far, (zsend, _) = swap(got), lax.optimization_barrier((zsend, got))
        zgot = swap(zsend)
        send, w, z, sw, rs, r, img, direct, sol, ist, known, kimg, scal, zsend = call(
            lambda *refs: next_kernel(zdim, xdim, first, last, *refs), f"step{iteration}",
            [ids, got, far, zgot, deflation, d_other, *dx, s_hi, s_lo, select, strips, *consts, known, w, z, sw, rs, *state],
            [(peers * nz, 1, LANES) if last else slots, brick, mine, (xdim, LANES), one, full, full, mine, mine, one,
             (tiles, LANES), (tiles, LANES), (8, LANES), (2, xdim, LANES)],
            scratch + [(zdim + 2, max(8, xdim // 4), LANES)], smem=1,
        )
        state = [r, img, direct, sol, ist, kimg, scal]
    got = lax.all_to_all(send, ("gx", "gy", "gz"), 0, 0, tiled=True)
    return tuple(call(
        lambda *refs: last_kernel(zdim, xdim, *refs), "last",
        [got, w, z, r, img, direct, sol, scal], [mine, mine],
    ))


def solution(mesh):
    in_specs = (
        P("gz", "gx", "gy"),
        P("gz", "gx", "gy"),
        P("gz", "gx", "gy"),
        P(None, "gz", "gx", "gy"),
        P("gx", None),
        P("gz", "gx", "gy", None),
        P("gz", "gx", "gy", None),
    )
    out_specs = (P("gz", "gx", "gy"), P("gz", "gx", "gy"))
    return jax.shard_map(local, mesh=mesh, in_specs=in_specs, out_specs=out_specs, check_vma=False)
```

```python
import jax
import jax.numpy as jnp
from jax import lax
from jax.experimental import pallas as pl
from jax.experimental.pallas import tpu as pltpu
from jax.sharding import PartitionSpec as P

ITERS = 4
RELAXATION = 0.7
PRECISE = lax.Precision.HIGHEST
LANES = 128
STRIDE = 8
PERIOD = 32


def conduct(first_perm, second_perm):
    return 2.0 * first_perm * second_perm / jnp.maximum(first_perm + second_perm, 0.05)


def turn(values, shift, axis):
    size = values.shape[axis]
    if isinstance(shift, int):
        shift = shift % size
        if shift == 0:
            return values
    return pltpu.roll(values, shift, axis)


def rem(a, b):
    return a % b if isinstance(a, int) else lax.rem(a, b)


def x_next(v):
    return turn(v, -1, 0)


def x_prev(v):
    return turn(v, 1, 0)


def y_next(v):
    return turn(v, -1, 1)


def y_prev(v):
    return turn(v, 1, 1)


def iota(shape, dim):
    return lax.broadcasted_iota(jnp.int32, shape, dim)


def place(shape):
    lane = iota(shape, 1)
    return lane >> 3, lane & 7


def mirror(p, zdim):
    return p + lax.axis_index("gz") * (zdim - 1 - 2 * p)


def by_tiles(mask, values, tiles):
    parts, at = [], 0
    for t in tiles:
        if 8 * t > at:
            parts.append(values[at : 8 * t])
        at = 8 * (t + 1)
        parts.append(mask[8 * t : at] * values[8 * t : at])
    if at < values.shape[0]:
        parts.append(values[at:])
    return jnp.concatenate(parts, axis=0)


def eights(values):
    out = values[0:8]
    for t in range(1, values.shape[0] // 8):
        out = out + values[8 * t : 8 * t + 8]
    return out


def spread_row(acc_ref):
    count = acc_ref.shape[0]
    column = jnp.broadcast_to(jnp.sum(acc_ref[...], axis=1, keepdims=True), (count, LANES))
    match = iota((count, LANES), 0) == (iota((count, LANES), 1) & (count - 1))
    return jnp.sum(jnp.where(match, column, 0.0), axis=0, keepdims=True)


def prep_kernel(zdim, xdim, perm, stor, resid, d, owners, margin, whole, row_ref, up_ref, down_ref, acc, line):
    for f, field in enumerate((perm, stor, resid)):
        for pz in range(zdim):
            at = (f * zdim + pz) * 3
            up_ref[at : at + 3, :] = field[mirror(pz, zdim), xdim - 3 : xdim, :]
            down_ref[at : at + 3, :] = field[mirror(pz, zdim), 0:3, :]
    vectors = d.shape[0]
    acc[...] = jnp.zeros(acc.shape, jnp.float32)
    for k in range(vectors):
        total = jnp.zeros((8, LANES), jnp.float32)
        for pz in range(zdim):
            at = (9 + k) * zdim + pz
            up_ref[at : at + 1, :] = d[k, mirror(pz, zdim), xdim - 1 : xdim, :]
            down_ref[at : at + 1, :] = d[k, mirror(pz, zdim), 0:1, :]
            total = total + eights(d[k, pz] * resid[pz])
        acc[k : k + 1, :] = jnp.sum(total, axis=0, keepdims=True)
    line[...] = jnp.zeros(line.shape, jnp.float32)
    line[0:1, 8 : 8 + vectors] = owners[...].astype(jnp.float32)
    line[0:1, 16:22] = margin[...].astype(jnp.float32)
    extra = line[0:1, :]
    extra = extra + turn(extra, PERIOD, 1)
    extra = extra + turn(extra, 2 * PERIOD, 1)
    row = spread_row(acc) + extra
    share, halves = row_ref.shape[1] - 1, row_ref.shape[2]
    block = lax.axis_index("gy") * lax.axis_size("gz") + lax.axis_index("gz")
    piece = whole[pl.ds(pl.multiple_of(block * share, 8), share), :]
    for p in range(row_ref.shape[0]):
        row_ref[p, share, 0:1, :] = row
        for h in range(halves):
            row_ref[p, 0:share, h, :] = piece[:, LANES * h : LANES * (h + 1)]


def coarse_kernel(ids, table, select, known_ref, near, hot, whole):
    order = whole.shape[0]
    share = table.shape[1] - 1
    for p in range(table.shape[0]):
        for h in range(table.shape[2]):
            whole[share * p : share * (p + 1), LANES * h : LANES * (h + 1)] = table[p, 0:share, h, :]
    zb = ids[9]
    place_of = (zb, 1 - zb)
    lane = iota((1, LANES), 1)
    lane8, sub8 = iota((8, LANES), 1), iota((8, LANES), 0)
    number = iota((8, order), 1).astype(jnp.float32)
    near[...] = jnp.zeros(near.shape, jnp.float32)
    for col in range(5):
        for b in range(2):
            row = table[2 * ids[col] + place_of[b], share, 0:1, :]
            near[2 * col + b : 2 * col + b + 1, :] = row
            owner = jnp.sum(jnp.where(lane8 == sub8 + 8, row, 0.0), axis=1, keepdims=True)
            at = 8 * (3 * b + col if col < 3 else 2 * col + b)
            hot[at : at + 8, :] = (number == owner).astype(jnp.float32)
    rows = jnp.dot(hot[...], whole[...], precision=PRECISE, preferred_element_type=jnp.float32)
    index = iota((order, LANES), 0).astype(jnp.float32)
    for t in range(known_ref.shape[0]):
        known = jnp.zeros((1, LANES), jnp.float32)
        owner = known - 1.0
        for i in range(4):
            for b in range(2):
                row = table[2 * (4 * t + i) + place_of[b], share, 0:1, :]
                mine = (lane >> 3) == 4 * i + b
                known = jnp.where(mine, turn(row, 8 * b, 1), known)
                owner = jnp.where(mine, turn(row, 8 * b - 8, 1), owner)
        known_ref[t : t + 1, :] = known
        pick = (index == owner).astype(jnp.float32)
        select[:, LANES * t : LANES * (t + 1)] = jnp.dot(
            rows, pick, precision=PRECISE, preferred_element_type=jnp.float32
        )


def plane_of_field(fields, halos, f, p):
    own, other = fields
    zdim, xdim = own[0].shape[0], own[0].shape[1]
    hi_own, lo_own, hi_other, lo_other = halos
    src, hi, lo = (own, hi_own, lo_own) if p < zdim else (other, hi_other, lo_other)
    at = (f * zdim + (p if p < zdim else 2 * zdim - 1 - p)) * 3
    gap = jnp.zeros((2, LANES), jnp.float32)
    tile = jnp.concatenate([hi[at : at + 3, :], gap, lo[at : at + 3, :]], axis=0)
    return jnp.concatenate([src[f][mirror(p % zdim, zdim)], tile], axis=0)


def pack_kernel(zdim, xdim, *refs):
    fields = (refs[0:3], refs[3:6])
    halos, d_own = refs[6:10], refs[10]
    strip_hi, strip_lo = refs[11:13]
    rows = xdim + 8
    shape = (rows, LANES)
    plane_of, slot_of = place(shape)
    for f in range(3):
        acc = jnp.zeros(shape, jnp.float32)
        for p in range(zdim + 3):
            moved = turn(plane_of_field(fields, halos, f, p), STRIDE * p + 3, 1)
            acc = jnp.where((plane_of == p) & (slot_of < 6), moved, acc)
        strip_hi[f * rows : (f + 1) * rows, :] = acc
        strip_lo[f * rows : (f + 1) * rows, :] = acc
    lane = iota((xdim, LANES), 1)
    vectors = d_own.shape[0]
    hi_acc = jnp.zeros((xdim, LANES), jnp.float32)
    lo_acc = hi_acc
    for k in range(vectors):
        for p in range(zdim):
            at = STRIDE * p + k
            moved = turn(d_own[k, mirror(p, zdim)], at + 1, 1)
            hi_acc = jnp.where(lane == at, moved, hi_acc)
            lo_acc = jnp.where(lane == at + 1, moved, lo_acc)
    strip_hi[3 * rows : 3 * rows + xdim, :] = hi_acc
    strip_lo[3 * rows : 3 * rows + xdim, :] = turn(lo_acc, -1, 1)


def solve_coarse(known, select_ref, yb_ref):
    total = 0.0
    for t, row in enumerate(known):
        total = total + select_ref[:, LANES * t : LANES * (t + 1)] * row
    column = jnp.sum(total, axis=1, keepdims=True)
    yb_ref[...] = jnp.broadcast_to(column, yb_ref.shape)


def finish(c, scaled, strip_q, r_ref, z_ref, send_ref, w_ref, zown_ref, sw_ref, zsend_ref, img_ref, ids, last):
    zdim, xdim = c["d_own"].shape[1], c["d_own"].shape[2]
    rows = xdim + 8
    vectors = c["d_own"].shape[0]
    strips = c["strips"]
    yb = c["yb"]
    plane_of, slot_of = place((rows, LANES))

    te, cxp, cxm, cin, cout, czp, czm, ss = (strips[i] for i in range(8))
    smooth = (
        cxp * x_next(strip_q)
        + cxm * x_prev(strip_q)
        + cin * turn(strip_q, 4, 1)
        + cout * turn(strip_q, 2, 1)
        + czp * turn(strip_q, -STRIDE, 1)
        + czm * turn(strip_q, STRIDE, 1)
    )
    strip_z = (2.0 - RELAXATION) * strip_q + ss * smooth
    lane8, row8 = iota((vectors, LANES), 1), iota((vectors, LANES), 0)
    wanted = row8 == (lane8 & 7)
    for side, d_strip in ((0, c["dy_hi"]), (1, c["dy_lo"])):
        at = 6 * vectors + side * 2 * vectors
        coeff = jnp.sum(jnp.where(wanted, yb[at : at + vectors, :], 0.0), axis=0, keepdims=True)
        t = d_strip[...] * coeff
        t = t + turn(t, -1, 1)
        t = t + turn(t, -2, 1)
        t = t + turn(t, -4, 1)
        t = jnp.where(slot_of[:xdim] == 5 + side, turn(t, 5 + side, 1), 0.0)
        t = jnp.concatenate([t, jnp.zeros((8, LANES), jnp.float32)], axis=0)
        strip_z = strip_z + t
    edge_q = te * strip_q
    edge_z = te * strip_z

    for side in range(2):
        dx = c["dx"][side]
        acc = 0.0
        for k in range(vectors):
            at = (1 + side) * vectors + k
            start = (9 + k) * zdim
            acc = acc + dx[start : start + zdim, :] * yb[at : at + 1, :]
        c["bx"][side] = acc
    row8 = iota((8, LANES), 0)
    nothing = jnp.zeros((8, LANES), jnp.float32)
    for p in range(zdim + 1):
        b = p // zdim
        d_ref = c["d_own"] if b == 0 else c["d_other"]
        mxp, mxm, my = c["mxp"][b], c["mxm"][b], c["my"][b]
        q = scaled[p]
        tx, ty = c["tx"][p], c["ty"][p]
        acc = by_tiles(mxp, tx * x_next(q), (xdim // 8 - 1, xdim // 8))
        acc = acc + by_tiles(mxm, x_prev(tx * q), (0, xdim // 8))
        acc = acc + ty * y_next(q) + y_prev(ty * q)
        acc = acc + my * turn(edge_q, LANES - 6 - STRIDE * p, 1)
        acc = acc + c["tzlp"][p] * scaled[p + 1]
        if p > 0:
            acc = acc + c["tzlm"][p] * scaled[p - 1]
        z = (2.0 - RELAXATION) * q + c["s"][p] * acc
        field = 0.0
        at = 3 * b * vectors
        for k in range(vectors):
            field = field + d_ref[k, mirror(p % zdim, zdim)] * yb[at + k : at + k + 1, :]
        tile = nothing
        if b == 0:
            tile = jnp.where(row8 == 0, c["bx"][0, p : p + 1, :], 0.0)
            tile = jnp.where(row8 == 7, c["bx"][1, p : p + 1, :], tile)
            zown_ref[p] = (z[:xdim] + field)
        z_ref[p] = z + jnp.concatenate([field, tile], axis=0)

    lane = iota((rows, LANES), 1)
    edge = jnp.where((lane == 0) | (lane == LANES - 1), 1.0, 0.0)
    plane64, slot64 = plane_of[:xdim], slot_of[:xdim]
    rz = zw = zi = nothing
    sums = [nothing] * vectors
    packed = jnp.zeros((xdim, LANES), jnp.float32)
    for p in range(zdim):
        z = z_ref[p]
        tx, ty = c["tx"][p], c["ty"][p]
        acc = tx * x_next(z) + x_prev(tx * z)
        acc = acc + ty * y_next(z) + y_prev(ty * z)
        acc = acc + edge * turn(edge_z, LANES - 6 - STRIDE * p, 1)
        acc = acc + c["tz"][p] * z_ref[p + 1]
        if p > 0:
            acc = acc + c["tz"][p - 1] * z_ref[p - 1]
        w = (c["diag"][p] * z - acc)[:xdim]
        z = z[:xdim]
        w_ref[p] = w
        rz = rz + eights(r_ref[p][:xdim] * z)
        zw = zw + eights(w * z)
        if img_ref is not None:
            zi = zi + eights(img_ref[p][:xdim] * z)
        if last:
            continue
        for k in range(vectors):
            sums[k] = sums[k] + eights(c["d_own"][k, mirror(p, zdim)] * w)
        moved = turn(w, STRIDE * p + 2, 1)
        packed = jnp.where((plane64 == p) & (slot64 < 4), moved, packed)

    acc_ref = c["acc"]
    acc_ref[...] = jnp.zeros(acc_ref.shape, jnp.float32)
    for j, value in list(enumerate(sums)) + [(16, rz), (17, zw), (18, zi)]:
        acc_ref[j : j + 1, :] = jnp.sum(value, axis=0, keepdims=True)
    row = spread_row(acc_ref)
    peers = send_ref.shape[0]
    if last:
        for p in range(peers):
            send_ref[p] = row
        return
    for p in range(peers):
        send_ref[p, zdim, 0:1, :] = row
    sw_ref[...] = packed
    zsend_ref[0] = w_ref[zdim - 1]
    zsend_ref[1] = w_ref[zdim - 2]
    for p in range(zdim):
        send_ref[ids[1], p] = w_ref[p, xdim - 2 : xdim, :]
        send_ref[ids[2], p] = w_ref[p, 0:2, :]
    part = xdim // 4
    pair = (iota((part, LANES), 1) & 7) >> 1
    to_hi = jnp.zeros((part, LANES), jnp.float32)
    to_lo = to_hi
    for g in range(4):
        rows_g = packed[g * part : (g + 1) * part]
        to_hi = jnp.where(pair == g, turn(rows_g, 2 * g, 1), to_hi)
        to_lo = jnp.where(pair == g, turn(rows_g, 2 * g - 2, 1), to_lo)
    for i in range(part // 2):
        send_ref[ids[3], i] = to_hi[2 * i : 2 * i + 2]
        send_ref[ids[4], i] = to_lo[2 * i : 2 * i + 2]
    for i in (5, 6):
        send_ref[ids[i], 0, 0:1, :] = packed[xdim - 1 : xdim, :]
    for i in (7, 8):
        send_ref[ids[i], 0, 0:1, :] = packed[0:1, :]


def first_kernel(zdim, xdim, *refs):
    (ids, near, s_own, s_hi, s_lo, d_own, d_other) = refs[0:7]
    dx = refs[7:11]
    (select, known_ref) = refs[11:13]
    fields = (refs[13:16], refs[16:19])
    refs = refs[19:]
    (send, w_ref, zown, sw, strips, tx, ty, tz, tzlp, tzlm, s_ref, diag_ref, mxp, mxm, my, rs_ref, r_full, zsend) = refs[:18]
    (scaled, z_ref, yb, acc, bx) = refs[18:23]
    rows = xdim + 8
    deep = zdim + 3
    shape = (rows, LANES)
    row, lane = iota(shape, 0), iota(shape, 1)
    plane_of, slot_of = place(shape)
    mirrored = ids[9] == 1

    def mg(col, b, d):
        at = 2 * col + b
        return near[at : at + 1, 16 + d : 17 + d]

    def facing(col, b, up):
        return jnp.where(mirrored, mg(col, b, 0 if up else 1), mg(col, b, 1 if up else 0))

    def z_by_row(b, up):
        beyond = jnp.where(row < xdim + 4, facing(1, b, up), facing(2, b, up))
        return jnp.where(row < xdim, facing(0, b, up), beyond)

    def by_row(b, d):
        return jnp.where(row < xdim, mg(0, b, d), jnp.where(row < xdim + 4, mg(1, b, d), mg(2, b, d)))

    for b in range(2):
        mxp[b] = jnp.where(row == xdim - 1, mg(0, b, 3), jnp.where(row == rows - 1, mg(2, b, 3), 1.0))
        mxm[b] = jnp.where(row == 0, mg(0, b, 2), jnp.where(row == xdim, mg(1, b, 2), 1.0))
        my[b] = jnp.where(lane == LANES - 1, by_row(b, 5), jnp.where(lane == 0, by_row(b, 4), 0.0))

    def strip(i):
        at = slice(i * rows, (i + 1) * rows)
        own, hi, lo = s_own[at, :], s_hi[at, :], s_lo[at, :]
        out = jnp.where((slot_of == 1) | (slot_of == 2), turn(own, -1, 1), 0.0)
        out = jnp.where(slot_of == 5, turn(hi, 2, 1), out)
        out = jnp.where(slot_of == 3, turn(hi, -1, 1), out)
        out = jnp.where(slot_of == 0, turn(hi, -5, 1), out)
        out = jnp.where(slot_of == 6, turn(lo, 4, 1), out)
        out = jnp.where(slot_of == 4, turn(lo, 3, 1), out)
        return jnp.where(slot_of == 7, turn(lo, 7, 1), out)

    ps, st, rs = strip(0), strip(1), strip(2)
    rs_ref[...] = rs
    face = (slot_of == 5) | (slot_of == 6)
    t_x = conduct(ps, x_next(ps))
    t_z = jnp.where(plane_of < deep - 1, conduct(ps, turn(ps, -STRIDE, 1)), 0.0)
    t_in = jnp.where(face, conduct(ps, turn(ps, 4, 1)), 0.0)
    t_out = jnp.where(face, conduct(ps, turn(ps, 2, 1)), 0.0)
    t_far = jnp.where(
        slot_of == 3,
        conduct(ps, turn(ps, 3, 1)),
        jnp.where(slot_of == 4, conduct(ps, turn(ps, -3, 1)), 0.0),
    )
    diag_s = st + t_x + x_prev(t_x) + t_z + turn(t_z, STRIDE, 1)
    diag_s = diag_s + t_in + t_out + turn(t_out, -2, 1) + t_far
    ss = jnp.where(diag_s > 0.0, RELAXATION / jnp.where(diag_s > 0.0, diag_s, 1.0), 0.0)

    def by_side(b, d_hi, d_lo):
        return jnp.where(slot_of == 5, mg(3, b, d_hi), mg(4, b, d_lo))

    def by_brick(d_hi, d_lo):
        return jnp.where(plane_of < zdim, by_side(0, d_hi, d_lo), by_side(1, d_hi, d_lo))

    def only(values):
        return jnp.where(face, values, 0.0)

    strips[0] = t_in
    strips[1] = only(t_x * jnp.where(row == xdim - 1, by_brick(3, 3), 1.0))
    strips[2] = only(x_prev(t_x) * jnp.where(row == 0, by_brick(2, 2), 1.0))
    strips[3] = t_in * by_brick(4, 5)
    strips[4] = t_out
    at_side = jnp.where(slot_of == 5, facing(3, 0, True), facing(4, 0, True))
    strips[5] = only(t_z * jnp.where(plane_of == zdim - 1, at_side, 1.0))
    strips[6] = only(jnp.where(plane_of == 0, 0.0, turn(t_z, STRIDE, 1)))

    inside = lane < LANES - 1

    for p in range(deep):
        scaled[p] = plane_of_field(fields, dx, 0, p)
        diag_ref[p] = plane_of_field(fields, dx, 1, p)
        r_full[p] = plane_of_field(fields, dx, 2, p)
    for p in range(deep - 1):
        here = scaled[p]
        tx[p] = conduct(here, x_next(here))
        ty[p] = jnp.where(inside, conduct(here, y_next(here)), 0.0)
        tz[p] = conduct(here, scaled[p + 1])
    edge = (lane == 0) | (lane == LANES - 1)
    inner = jnp.zeros(shape, jnp.float32)
    for p in range(deep - 1):
        t_x, t_y, t_z = tx[p], ty[p], tz[p]
        t_b = tz[p - 1] if p > 0 else jnp.zeros(shape, jnp.float32)
        total = diag_ref[p] + t_x + x_prev(t_x) + t_y + y_prev(t_y) + t_z + t_b
        total = total + jnp.where(edge, turn(t_in, LANES - 6 - STRIDE * p, 1), 0.0)
        relax = jnp.where(total > 0.0, RELAXATION / jnp.where(total > 0.0, total, 1.0), 0.0)
        diag_ref[p] = total
        s_ref[p] = relax
        tzlp[p] = t_z * z_by_row(0, True) if p == zdim - 1 else t_z
        tzlm[p] = t_b * z_by_row(1, False) if p == zdim else t_b
        scaled[p] = relax * r_full[p]
        if p < zdim:
            moved = turn(relax, STRIDE * p + 2, 1)
            inner = jnp.where((plane_of == p) & ((slot_of == 1) | (slot_of == 2)), moved, inner)
    ss = jnp.where((slot_of == 1) | (slot_of == 2), inner, ss)
    strips[7] = ss

    known = [known_ref[t : t + 1, :] for t in range(known_ref.shape[0])]
    solve_coarse(known, select, yb)
    c = dict(
        tx=tx, ty=ty, tz=tz, tzlp=tzlp, tzlm=tzlm, s=s_ref, diag=diag_ref, mxp=mxp, mxm=mxm, my=my,
        strips=strips, d_own=d_own, d_other=d_other, dx=dx, dy_hi=s_hi.at[3 * rows : 3 * rows + xdim, :],
        dy_lo=s_lo.at[3 * rows : 3 * rows + xdim, :], yb=yb, acc=acc, bx=bx,
    )
    finish(c, scaled, ss * rs, r_full, z_ref, send, w_ref, zown, sw, zsend, None, ids, False)


def totals(rows, count):
    lane = iota((1, LANES), 1)
    total = 0.0
    for i in range(count):
        total = total + (rows(i, 0) + rows(i, 1))
    sums = [
        jnp.sum(jnp.where(lane == 16 + j, total, 0.0), axis=1, keepdims=True) for j in range(3)
    ]
    tiles = []
    for t in range(count // 4):
        tile = jnp.zeros((1, LANES), jnp.float32)
        for i in range(4):
            for b in range(2):
                mine = (lane >> 3) == 4 * i + b
                tile = jnp.where(mine, turn(rows(4 * t + i, b), 8 * b, 1), tile)
        tiles.append(tile)
    return tiles, sums


def scalars(sums, scal_ref, first):
    inner = sums[0]
    if first:
        ratio = jnp.zeros_like(inner)
        curvature = sums[1]
    else:
        ratio = inner / scal_ref[0:1, 0:1]
        curvature = sums[1] + ratio * (2.0 * sums[2] + ratio * scal_ref[1:2, 0:1])
    return inner, ratio, curvature, inner / curvature


def next_kernel(zdim, xdim, first, last, *refs):
    refs = list(refs)

    def take(n):
        out, refs[:n] = refs[:n], []
        return out

    ids, got, far, zgot, d_own, d_other, *dx = take(10)
    s_hi, s_lo, select, strips, tx, ty, tz, tzlp, tzlm, s_ref, diag_ref, mxp, mxm, my = take(14)
    known_ref, w_in, z_in, sw_in, rs_in = take(5)
    if first:
        (r_in,) = take(1)
    else:
        r_in, img_in, dir_in, sol_in, is_in, kimg_ref, scal_ref = take(7)
    send, w_ref, zown, sw, rs_ref, r_ref, img_ref, dir_ref, sol_ref, is_ref, known_out, kimg_out, scal_out, zsend = take(14)
    scaled, z_ref, yb, acc, bx, tiles_ref = take(6)
    rows = xdim + 8
    plane_of, slot_of = place((rows, LANES))

    peers = got.shape[0]
    tiles, sums = totals(lambda i, b: (got, far)[b][i, zdim, 0:1, :], peers)
    inner, ratio, curvature, step = scalars(sums, None if first else scal_ref, first)
    scal_out[0:1, :] = jnp.broadcast_to(inner, (1, LANES))
    scal_out[1:2, :] = jnp.broadcast_to(curvature, (1, LANES))
    known = []
    for t, tile in enumerate(tiles):
        if not first:
            tile = tile + ratio * kimg_ref[t : t + 1, :]
        kimg_out[t : t + 1, :] = tile
        value = known_ref[t : t + 1, :] - step * tile
        known_out[t : t + 1, :] = value
        known.append(value)
    solve_coarse(known, select, yb)

    part = xdim // 4
    for i in range(part // 2):
        for j in range(4):
            tiles_ref[j, 2 * i : 2 * i + 2, :] = (got, far)[j // 2][ids[3 + j % 2], i]
    from_hi, from_lo, far_hi, far_lo = (tiles_ref[j] for j in range(4))
    beyond = plane_of[:part] == zdim
    own = sw_in[...]
    slot_part = slot_of[:part]
    blocks = []
    for g in range(4):
        value = own[g * part : (g + 1) * part]
        value = jnp.where(slot_part == 5, turn(from_hi, 5 - 2 * g, 1), value)
        value = jnp.where(slot_part == 3, turn(from_hi, 2 - 2 * g, 1), value)
        value = jnp.where(slot_part == 4, turn(from_lo, 4 - 2 * g, 1), value)
        value = jnp.where(slot_part == 6, turn(from_lo, 5 - 2 * g, 1), value)
        value = jnp.where(beyond & (slot_part == 5), turn(far_hi, STRIDE + 5 - 2 * g, 1), value)
        value = jnp.where(beyond & (slot_part == 6), turn(far_lo, STRIDE + 5 - 2 * g, 1), value)
        blocks.append(value)
    slot8, row8 = slot_of[:8], iota((8, LANES), 0)
    tile = jnp.zeros((8, LANES), jnp.float32)
    for i, at, want, shift in ((5, 0, 5, 3), (6, 0, 6, 5), (7, 7, 5, 3), (8, 7, 6, 5)):
        value = turn(jnp.broadcast_to(got[ids[i], 0, 0:1, :], (8, LANES)), shift, 1)
        tile = jnp.where((row8 == at) & (slot8 == want), value, tile)
    ws = jnp.concatenate(blocks + [tile], axis=0)
    ws = jnp.where((slot_of == 0) | (slot_of == 7), 0.0, ws)
    if not first:
        ws = ws + ratio * is_in[...]
    is_ref[...] = ws
    rs = rs_in[...] - step * ws
    rs_ref[...] = rs
    strip_q = strips[7] * rs

    tiles_ref[...] = jnp.zeros(tiles_ref.shape, jnp.float32)
    for p in range(zdim):
        tiles_ref[p, 0:2, :] = got[ids[1], p]
        tiles_ref[p, 6:8, :] = got[ids[2], p]
    tiles_ref[zdim, 0:1, :] = far[ids[1], zdim - 1, 0:1, :]
    tiles_ref[zdim, 7:8, :] = far[ids[2], zdim - 1, 1:2, :]
    for p in range(zdim + 2):
        inside = w_in[p] if p < zdim else zgot[p - zdim]
        image = jnp.concatenate([inside, tiles_ref[p, 0:8, :]], axis=0)
        if not first:
            image = image + ratio * img_in[p]
        img_ref[p] = image
        r = r_in[p] - step * image
        r_ref[p] = r
        scaled[p] = s_ref[p] * r
    for p in range(zdim):
        d = z_in[p]
        if first:
            sol_ref[p] = step * d
        else:
            d = d + ratio * dir_in[p]
            sol_ref[p] = sol_in[p] + step * d
        dir_ref[p] = d
    c = dict(
        tx=tx, ty=ty, tz=tz, tzlp=tzlp, tzlm=tzlm, s=s_ref, diag=diag_ref, mxp=mxp, mxm=mxm, my=my,
        strips=strips, d_own=d_own, d_other=d_other, dx=dx, dy_hi=s_hi.at[3 * rows : 3 * rows + xdim, :],
        dy_lo=s_lo.at[3 * rows : 3 * rows + xdim, :], yb=yb, acc=acc, bx=bx,
    )
    finish(c, scaled, strip_q, r_ref, z_ref, send, w_ref, zown, sw, zsend, img_ref, ids, last)


def last_kernel(zdim, xdim, got, w_in, z_in, r_in, img_in, dir_in, sol_in, scal_ref, sol_ref, r_ref):
    _, sums = totals(lambda i, b: got[2 * i + b], got.shape[0] // 2)
    _, ratio, _, step = scalars(sums, scal_ref, False)
    for p in range(zdim):
        at = mirror(p, zdim)
        image = w_in[p] + ratio * img_in[p][:xdim]
        r_ref[at] = r_in[p][:xdim] - step * image
        sol_ref[at] = sol_in[p] + step * (z_in[p] + ratio * dir_in[p])


def call(kernel, name, args, outs, scratch=(), smem=0, limit=24):
    specs = [pl.BlockSpec(memory_space=pltpu.SMEM)] * smem
    specs += [pl.BlockSpec(memory_space=pltpu.VMEM)] * (len(args) - smem)
    return pl.pallas_call(
        kernel,
        name=name,
        in_specs=specs,
        out_specs=[pl.BlockSpec(memory_space=pltpu.VMEM)] * len(outs),
        out_shape=[jax.ShapeDtypeStruct(o, jnp.float32) for o in outs],
        scratch_shapes=[pltpu.VMEM(s, jnp.float32) for s in scratch],
        compiler_params=pltpu.CompilerParams(vmem_limit_bytes=limit * 1024 * 1024),
    )(*args)


def local(right_side, permeability, storage, deflation, coarse_inverse, owners, margin):
    nx, ny, nz = (lax.axis_size(a) for a in ("gx", "gy", "gz"))
    vectors, zdim, xdim, ydim = deflation.shape
    order = coarse_inverse.shape[1]
    assert nz == 2 and ydim == LANES and 2 * zdim * STRIDE == LANES and vectors == 8
    gx, gy, gz = (lax.axis_index(a) for a in ("gx", "gy", "gz"))
    peers, rows = nx * ny, xdim + 8
    me = gx * ny + gy
    off_x = jnp.array([0, 1, -1, 0, 0, 1, 1, -1, -1, 0], jnp.int32) + gx
    off_y = jnp.array([0, 0, 0, 1, -1, 1, -1, 1, -1, 0], jnp.int32) + gy
    there = (off_x >= 0) & (off_x < nx) & (off_y >= 0) & (off_y < ny)
    ids = jnp.where(there, off_x * ny + off_y, me)
    ids = jnp.where(jnp.arange(10) == 9, gz, ids)

    def swap(v):
        return lax.ppermute(v, "gz", [(0, 1), (1, 0)])

    def up(v, axis, count):
        return lax.ppermute(v, axis, [(i, i + 1) for i in range(count - 1)])

    def down(v, axis, count):
        return lax.ppermute(v, axis, [(i + 1, i) for i in range(count - 1)])

    fields = (permeability, storage, right_side)
    others = [swap(v) for v in fields]
    d_other = swap(deflation)
    edge_rows = ((9 + vectors) * zdim, LANES)
    share = coarse_inverse.shape[0] // (ny * nz)
    assert share % 8 == 0
    first_row, x_up, x_down = call(
        lambda *refs: prep_kernel(zdim, xdim, *refs), "prep",
        [*fields, deflation, owners.reshape(1, -1), margin.reshape(1, -1), coarse_inverse],
        [(peers * nz, share + 1, order // LANES, LANES), edge_rows, edge_rows],
        [(PERIOD, LANES), (8, LANES)],
        limit=60,
    )
    x_lo, x_hi = up(x_up, "gx", nx), down(x_down, "gx", nx)
    table = lax.all_to_all(first_row, ("gx", "gy", "gz"), 0, 0, tiled=True)
    x_hi, x_lo = lax.optimization_barrier((x_hi, x_lo))
    dx = [x_hi, x_lo, swap(x_hi), swap(x_lo)]
    strip_rows = 3 * rows + xdim
    strip_hi, strip_lo = call(
        lambda *refs: pack_kernel(zdim, xdim, *refs), "pack",
        [*fields, *others, *dx, deflation],
        [(strip_rows, LANES), (strip_rows, LANES)],
    )
    s_lo = up(strip_hi, "gy", ny)
    s_hi = down(strip_lo, "gy", ny)
    tiles = peers * PERIOD // LANES
    select, known, near = call(
        coarse_kernel, "coarse", [ids, table],
        [(10 * vectors, peers * PERIOD), (tiles, LANES), (16, LANES)],
        [(10 * vectors, order), (order, order)], smem=1,
    )
    full, brick, one = (zdim + 3, rows, LANES), (zdim, xdim, LANES), (rows, LANES)
    mine, slots = (zdim, xdim, LANES), (peers, zdim + 1, 2, LANES)
    scratch = [full, full, (10 * vectors, LANES), (PERIOD, LANES), (2, zdim, LANES)]
    (send, w, z, sw, strips, *consts, rs, r_full, zsend) = call(
        lambda *refs: first_kernel(zdim, xdim, *refs), "first",
        [ids, near, strip_hi, s_hi, s_lo, deflation, d_other, *dx, select, known, *fields, *others],
        [slots, brick, mine, (xdim, LANES), (8, *one)] + [full] * 7 + [(2, *one)] * 3 + [one, full, (2, xdim, LANES)],
        scratch, smem=1,
    )
    state = [r_full]
    for iteration in range(ITERS - 1):
        first, last = iteration == 0, iteration == ITERS - 2
        got = lax.all_to_all(send, ("gx", "gy"), 0, 0, tiled=True)
        far, (zsend, _) = swap(got), lax.optimization_barrier((zsend, got))
        zgot = swap(zsend)
        send, w, z, sw, rs, r, img, direct, sol, ist, known, kimg, scal, zsend = call(
            lambda *refs: next_kernel(zdim, xdim, first, last, *refs), f"step{iteration}",
            [ids, got, far, zgot, deflation, d_other, *dx, s_hi, s_lo, select, strips, *consts, known, w, z, sw, rs, *state],
            [(peers * nz, 1, LANES) if last else slots, brick, mine, (xdim, LANES), one, full, full, mine, mine, one,
             (tiles, LANES), (tiles, LANES), (8, LANES), (2, xdim, LANES)],
            scratch + [(zdim + 2, max(8, xdim // 4), LANES)], smem=1,
        )
        state = [r, img, direct, sol, ist, kimg, scal]
    got = lax.all_to_all(send, ("gx", "gy", "gz"), 0, 0, tiled=True)
    return tuple(call(
        lambda *refs: last_kernel(zdim, xdim, *refs), "last",
        [got, w, z, r, img, direct, sol, scal], [mine, mine],
    ))


def solution(mesh):
    in_specs = (
        P("gz", "gx", "gy"),
        P("gz", "gx", "gy"),
        P("gz", "gx", "gy"),
        P(None, "gz", "gx", "gy"),
        P("gx", None),
        P("gz", "gx", "gy", None),
        P("gz", "gx", "gy", None),
    )
    out_specs = (P("gz", "gx", "gy"), P("gz", "gx", "gy"))
    return jax.shard_map(local, mesh=mesh, in_specs=in_specs, out_specs=out_specs, check_vma=False)
```
